256 devices in a mesh: dp: 8 (over z), seq: 32 (over x, y, core).
Axes of the slice: x: 4, y: 4, z: 8, core: 2. Of those that a mesh axis runs over, the one named last changes fastest.
Arguments:
- latents: bfloat16 [128, 2048], P(None, 'seq'), may hold values from -6 to 6
- saved_keys: bfloat16 [8, 24576, 2048], P('dp', 'seq'), may hold values from -6 to 6
- saved_values: bfloat16 [8, 24576, 2048], P('dp', 'seq'), may hold values from -6 to 6
- out_grad: bfloat16 [8, 128, 2048], P('dp', None, 'seq'), may hold values from -24576 to 24576, as said below
- out_saved: bfloat16 [8, 128, 2048], P('dp', None, 'seq'), may hold values from -6 to 6
- log_norm: float32 [8, 16, 128], P('dp'), as said below
Outputs:
- latent_grad: float32 [128, 2048], P(None, 'seq')
- key_grad: bfloat16 [8, 24576, 2048], P('dp', 'seq')
- value_grad: bfloat16 [8, 24576, 2048], P('dp', 'seq')
The draws below stay inside these ranges and needn't reach their ends.
Inputs may be any that keep to these rules, and one draw needn't show every extreme that they name: `log_norm`: each entry lies between the natural logarithm of 24576 minus 0.5 and that logarithm plus 1.5. `out_grad`: entries have magnitudes of order 24576 / 16 and lie within plus or minus 24576.
All inputs are finite; a program needn't handle non-finite values.
Results may differ from the reference program's by a relative error of at most 0.0015.
The reference program's roundings to bfloat16 on the way (of `weights_low` and `score_grad`) count: a program that leaves them out, or rounds other values in their place, can miss the bound.
Values may be sent and summed in bfloat16 or wider, within the bound.
A program may use at most 64 MiB of HBM per device.

```python
import math
import jax
import jax.numpy as jnp
from jax import lax

D = 2048
HEADS = 16
HEAD_DIM = 128
LATENTS = 128
TOKENS = 24576
EPISODES = 8


def draw_log_norm(key, part):
    centre = math.log(TOKENS) + 0.5
    shape = (EPISODES, HEADS, LATENTS)
    offsets = jax.random.uniform(key, shape, jnp.float32, -1.0, 1.0)
    return (centre + offsets).astype(jnp.float32)


def draw_out_grad(key, part):
    shape = (EPISODES, LATENTS, D)
    base = TOKENS / 16.0
    steps = jnp.arange(EPISODES, dtype=jnp.float32) / max(EPISODES - 1, 1)
    episode_scale = base * jnp.exp(steps * math.log(3.0))
    values = jax.random.normal(key, shape, jnp.float32) * episode_scale[:, None, None]
    return jnp.clip(values, -TOKENS * 1.0, TOKENS * 1.0).astype(jnp.bfloat16)


def block_levels(key, dims, split, low, largest):
    factor_of, own = 1.0, jax.random.fold_in(key, 6)
    for axis_at, shards_of in split:
        heights = jnp.exp(jax.random.uniform(jax.random.fold_in(own, axis_at), (shards_of,), jnp.float32, low / len(split), largest / len(split)))
        factor_of = factor_of * jnp.repeat(heights, dims[axis_at] // shards_of).reshape([-1 if axis == axis_at else 1 for axis in range(len(dims))])
    return factor_of


def bell_draw(stream_key, dims, width, reach, split=(), kind=jnp.bfloat16):
    entries = jax.random.normal(stream_key, dims, jnp.float32) * width
    if len(split) > 0:
        entries = block_levels(stream_key, dims, split, -0.22, 0.18) * entries
    return jnp.clip(entries, min=-reach, max=reach).astype(kind)


def setup_inputs(seed: int = 0) -> dict:
    seeds = jax.random.split(jax.random.key(seed), 7)
    latents = bell_draw(seeds[0], (LATENTS, D), 1.0, 6.0, ((1, 32),))
    saved_keys = bell_draw(seeds[1], (EPISODES, TOKENS, D), 1.0, 6.0, ((0, 8), (1, 32)))
    saved_values = bell_draw(seeds[2], (EPISODES, TOKENS, D), 1.0, 6.0, ((0, 8), (1, 32)))
    out_grad = draw_out_grad(jax.random.fold_in(seeds[6], 71), 0)
    out_saved = bell_draw(seeds[4], (EPISODES, LATENTS, D), 1.0, 6.0, ((0, 8), (2, 32)))
    log_norm = draw_log_norm(jax.random.fold_in(seeds[6], 71), 0)
    return {"latents": latents, "saved_keys": saved_keys, "saved_values": saved_values, "out_grad": out_grad, "out_saved": out_saved, "log_norm": log_norm}


def reference(latents, saved_keys, saved_values, out_grad, out_saved, log_norm):
    score_scale = HEAD_DIM ** -0.5
    query_heads = latents.astype(jnp.float32).reshape(LATENTS, HEADS, HEAD_DIM)

    def episode(episode_data):
        key_rows, value_rows, grad_rows, saved_rows, log_rows = episode_data
        key_heads = key_rows.astype(jnp.float32).reshape(TOKENS, HEADS, HEAD_DIM)
        value_heads = value_rows.astype(jnp.float32).reshape(TOKENS, HEADS, HEAD_DIM)
        grad_heads = grad_rows.astype(jnp.float32).reshape(LATENTS, HEADS, HEAD_DIM)
        saved_heads = saved_rows.astype(jnp.float32).reshape(LATENTS, HEADS, HEAD_DIM)
        row_dots = jnp.sum(grad_heads * saved_heads, axis=2).T
        scores = jnp.einsum("lhc,thc->hlt", query_heads, key_heads) * score_scale
        weights = jnp.exp(scores - log_rows[:, :, None])
        weights_low = lax.optimization_barrier(weights.astype(jnp.bfloat16)).astype(jnp.float32)
        value_grad = jnp.einsum("hlt,lhc->thc", weights_low, grad_heads)
        weight_grad = jnp.einsum("lhc,thc->hlt", grad_heads, value_heads)
        score_grad = score_scale * weights * (weight_grad - row_dots[:, :, None])
        score_low = lax.optimization_barrier(score_grad.astype(jnp.bfloat16)).astype(jnp.float32)
        key_grad = jnp.einsum("hlt,lhc->thc", score_low, query_heads)
        query_part = jnp.einsum("hlt,thc->lhc", score_low, key_heads).reshape(LATENTS, D)
        return (query_part,
                key_grad.reshape(TOKENS, D).astype(jnp.bfloat16),
                value_grad.reshape(TOKENS, D).astype(jnp.bfloat16))

    query_parts, key_grad, value_grad = lax.map(episode, (saved_keys, saved_values, out_grad, out_saved, log_norm))
    latent_grad = jnp.sum(query_parts, axis=0)
    return latent_grad, key_grad, value_grad
```

```python
import jax
import jax.numpy as jnp
from jax import lax
from jax.experimental import pallas as pl
from jax.experimental.pallas import tpu as pltpu
from jax.sharding import PartitionSpec as P

HEADS = 16
DIM = 128
LATENTS = 128
HALF = DIM // 2
SCALE = DIM ** (-0.5)
LOG2E = 1.4426950408889634
SIDE = 4
CHIPS = SIDE * SIDE
DEPTH = 8
ROWS = 2 * HALF + 16
MESH = pl.DeviceIdType.MESH
BF16 = jnp.bfloat16
F32 = jnp.float32

ORDER = (
    (0, 0), (0, 1), (0, 3), (1, 0), (3, 0), (1, 1), (3, 3), (1, 3),
    (3, 1), (0, 2), (2, 0), (1, 2), (3, 2), (2, 1), (2, 3), (2, 2),
)


def packed_codes(part):
    word = 0
    for at, (dx, dy) in enumerate(part):
        word |= (dx * SIDE + dy) << (4 * at)
    return word - (1 << 32) if word >= 1 << 31 else word


LOW, HIGH = packed_codes(ORDER[:8]), packed_codes(ORDER[8:])


def matmul(a, b, a_dim, b_dim):
    return lax.dot_general(
        a, b, (((a_dim,), (b_dim,)), ((), ())), preferred_element_type=F32
    )


def kernel(
    latents, keys, values, out_grad, out_saved, log_norm,
    share, key_grad, value_grad,
    kb, vb, saved, norms, pack, part, pair_in, pair_sum, reduce_in, z_in,
    local_sem, direct_send, direct_recv, forward_send, forward_recv,
    pair_send, pair_recv, reduce_send, reduce_recv, z_send, z_recv,
):
    z = lax.axis_index("dp")
    seat = lax.axis_index("seq")
    core = seat % 2
    chip = seat // 2
    x, y = chip // SIDE, chip % SIDE
    other = (z, chip * 2 + (1 - core))

    def behind(step):
        word = jnp.where(step < 8, jnp.int32(LOW), jnp.int32(HIGH))
        code = lax.shift_right_logical(word, (step % 8) * 4) % 16
        code = (code + 16) % 16
        return ((x + SIDE - code // SIDE) % SIDE) * SIDE + (y + SIDE - code % SIDE) % SIDE

    def ahead(dx, dy):
        return ((x + dx) % SIDE) * SIDE + (y + dy) % SIDE

    def seat_of(a_chip):
        return (z, a_chip * 2 + core)

    mine = pack.at[chip, core]
    local = [
        pltpu.make_async_copy(latents, mine.at[pl.ds(0, HALF)], local_sem.at[0]),
        pltpu.make_async_copy(out_grad, mine.at[pl.ds(HALF, HALF)], local_sem.at[1]),
        pltpu.make_async_copy(out_saved, saved, local_sem.at[2]),
        pltpu.make_async_copy(log_norm, norms, local_sem.at[3]),
        pltpu.make_async_copy(keys, kb, local_sem.at[4]),
        pltpu.make_async_copy(values, vb, local_sem.at[5]),
    ]
    for copy in local:
        copy.start()

    barrier = pltpu.get_barrier_semaphore()
    for dx, dy in ORDER[1:]:
        pl.semaphore_signal(barrier, inc=1, device_id=seat_of(ahead(dx, dy)), device_id_type=MESH)
    pl.semaphore_signal(barrier, inc=1, device_id=other, device_id_type=MESH)
    for dz in range(1, DEPTH):
        pl.semaphore_signal(barrier, inc=1, device_id=((z + dz) % DEPTH, seat), device_id_type=MESH)

    for copy in local[:3]:
        copy.wait()
    grads = pack[chip, core, HALF : 2 * HALF, :].astype(F32)
    dots = jnp.sum(grads * saved[...].astype(F32), axis=0, keepdims=True)
    top = dots.astype(BF16).astype(F32)
    middle = (dots - top).astype(BF16).astype(F32)
    rest = dots - top - middle
    row = lax.broadcasted_iota(jnp.int32, (16, DIM), 0)
    rows = jnp.where(row == 0, top, jnp.where(row == 1, middle, jnp.where(row == 2, rest, 0.0)))
    pack[chip, core, 2 * HALF : ROWS, :] = rows.astype(BF16)

    pl.semaphore_wait(barrier, CHIPS - 1 + 1 + DEPTH - 1)

    def direct(to):
        return pltpu.make_async_remote_copy(
            src_ref=mine, dst_ref=mine,
            send_sem=direct_send.at[to], recv_sem=direct_recv.at[chip],
            device_id=seat_of(to), device_id_type=MESH,
        )

    def direct_from(head):
        return pltpu.make_async_remote_copy(
            src_ref=mine, dst_ref=pack.at[head, core],
            send_sem=direct_send.at[head], recv_sem=direct_recv.at[head],
            device_id=seat_of(head), device_id_type=MESH,
        )

    def forward(head):
        return pltpu.make_async_remote_copy(
            src_ref=pack.at[head, core], dst_ref=pack.at[head, core],
            send_sem=forward_send.at[head], recv_sem=forward_recv.at[head],
            device_id=other, device_id_type=MESH,
        )

    def forward_from(head):
        return pltpu.make_async_remote_copy(
            src_ref=pack.at[head, core], dst_ref=pack.at[head, 1 - core],
            send_sem=forward_send.at[head], recv_sem=forward_recv.at[head],
            device_id=other, device_id_type=MESH,
        )

    def pair(head):
        return pltpu.make_async_remote_copy(
            src_ref=part.at[head, 1 - core], dst_ref=pair_in.at[head],
            send_sem=pair_send.at[head], recv_sem=pair_recv.at[head],
            device_id=other, device_id_type=MESH,
        )

    def reduce(head):
        return pltpu.make_async_remote_copy(
            src_ref=pair_sum.at[head], dst_ref=reduce_in.at[chip],
            send_sem=reduce_send.at[head], recv_sem=reduce_recv.at[chip],
            device_id=seat_of(head), device_id_type=MESH,
        )

    def reduce_from(head):
        return pltpu.make_async_remote_copy(
            src_ref=pair_sum.at[head], dst_ref=reduce_in.at[head],
            send_sem=reduce_send.at[head], recv_sem=reduce_recv.at[head],
            device_id=seat_of(head), device_id_type=MESH,
        )

    forward(chip).start()
    for dx, dy in ORDER[1:]:
        direct(ahead(dx, dy)).start()
    for copy in local[3:]:
        copy.wait()

    def combine(head):
        pair(head).wait_recv()
        pair_sum[head] = part[head, core] + pair_in[head]

    def meet(step, carry):
        head = behind(step)

        @pl.when(step < CHIPS - 1)
        def _():
            following = behind(step + 1)
            direct_from(following).wait_recv()
            forward(following).start()

        forward_from(head).wait_recv()
        columns = pl.ds(pl.multiple_of(head * DIM, DIM), DIM)
        query = jnp.concatenate([pack[head, 0, :HALF, :], pack[head, 1, :HALF, :]], axis=0)
        grad = jnp.concatenate(
            [pack[head, 0, HALF : 2 * HALF, :], pack[head, 1, HALF : 2 * HALF, :]], axis=0
        )
        dot_rows = pack[head, 0, 2 * HALF : ROWS, :].astype(F32)
        dot_rows += pack[head, 1, 2 * HALF : ROWS, :].astype(F32)
        row_dots = jnp.sum(dot_rows, axis=0, keepdims=True)
        norm = norms[pl.ds(head, 1), :] * LOG2E
        key = kb[:, columns]
        scores = matmul(key, query, 1, 0)
        weight_grad = matmul(vb[:, columns], grad, 1, 0)
        weights = jnp.exp2(scores * (SCALE * LOG2E) - norm)
        score_low = ((SCALE * weights) * (weight_grad - row_dots)).astype(BF16)
        terms = matmul(key, score_low, 0, 0)
        part[head, 0] = terms[:HALF]
        part[head, 1] = terms[HALF:]
        pair(head).start()
        value_grad[:, columns] = matmul(weights.astype(BF16), grad, 1, 1).astype(BF16)
        key_grad[:, columns] = matmul(score_low, query, 1, 1).astype(BF16)

        @pl.when(step >= 1)
        def _():
            before = behind(jnp.maximum(step - 1, 0))
            combine(before)

            @pl.when(step >= 2)
            def _():
                reduce(before).start()

        return carry

    lax.fori_loop(0, CHIPS, meet, 0)
    last = behind(jnp.int32(CHIPS - 1))
    combine(last)
    reduce(last).start()

    total = pair_sum[chip]
    for dx, dy in ORDER[1:]:
        sender = ahead(dx, dy)
        reduce_from(sender).wait_recv()
        total += reduce_in[sender]
    z_in[z] = total

    def cross(to):
        return pltpu.make_async_remote_copy(
            src_ref=z_in.at[z], dst_ref=z_in.at[z],
            send_sem=z_send.at[to], recv_sem=z_recv.at[z],
            device_id=(to, seat), device_id_type=MESH,
        )

    def cross_from(sender):
        return pltpu.make_async_remote_copy(
            src_ref=z_in.at[z], dst_ref=z_in.at[sender],
            send_sem=z_send.at[sender], recv_sem=z_recv.at[sender],
            device_id=(sender, seat), device_id_type=MESH,
        )

    for dz in (4, 3, 5, 2, 6, 1, 7):
        cross((z + dz) % DEPTH).start()
    for dz in (1, 7, 2, 6, 3, 5, 4):
        cross_from((z + dz) % DEPTH).wait_recv()
    result = z_in[0]
    for at in range(1, DEPTH):
        result += z_in[at]
    share[...] = result

    forward(chip).wait_send()
    pair(chip).wait_send()
    for dx, dy in ORDER[1:]:
        to = ahead(dx, dy)
        direct(to).wait_send()
        forward(to).wait_send()
        pair(to).wait_send()
        reduce(to).wait_send()
    for dz in range(1, DEPTH):
        cross((z + dz) % DEPTH).wait_send()


def local(latents, saved_keys, saved_values, out_grad, out_saved, log_norm):
    tokens, width = saved_keys.shape[1:]
    dma = pltpu.SemaphoreType.DMA
    hbm = pl.BlockSpec(memory_space=pltpu.MemorySpace.HBM)
    vmem = pl.BlockSpec(memory_space=pltpu.MemorySpace.VMEM)
    share, key_grad, value_grad = pl.pallas_call(
        kernel,
        name="resampler_backward",
        out_shape=(
            jax.ShapeDtypeStruct((HALF, LATENTS), F32),
            jax.ShapeDtypeStruct((tokens, width), BF16),
            jax.ShapeDtypeStruct((tokens, width), BF16),
        ),
        in_specs=[hbm] * 6,
        out_specs=(vmem, vmem, vmem),
        scratch_shapes=[
            pltpu.VMEM((tokens, width), BF16),
            pltpu.VMEM((tokens, width), BF16),
            pltpu.VMEM((HALF, LATENTS), BF16),
            pltpu.VMEM((HEADS, LATENTS), F32),
            pltpu.VMEM((CHIPS, 2, ROWS, LATENTS), BF16),
            pltpu.VMEM((CHIPS, 2, HALF, LATENTS), F32),
            pltpu.VMEM((CHIPS, HALF, LATENTS), F32),
            pltpu.VMEM((CHIPS, HALF, LATENTS), F32),
            pltpu.VMEM((CHIPS, HALF, LATENTS), F32),
            pltpu.VMEM((DEPTH, HALF, LATENTS), F32),
            dma((6,)),
            dma((CHIPS,)), dma((CHIPS,)), dma((CHIPS,)), dma((CHIPS,)),
            dma((CHIPS,)), dma((CHIPS,)), dma((CHIPS,)), dma((CHIPS,)),
            dma((DEPTH,)), dma((DEPTH,)),
        ],
        compiler_params=pltpu.CompilerParams(
            collective_id=0, has_side_effects=True, vmem_limit_bytes=40 << 20
        ),
    )(
        *(pltpu.with_memory_space_constraint(a, pltpu.MemorySpace.HBM) for a in (latents.T, saved_keys[0], saved_values[0], out_grad[0].T, out_saved[0].T, log_norm[0]))
    )
    return share.T, key_grad[None], value_grad[None]


def solution(mesh):
    placed = (
        P(None, "seq"),
        P("dp", "seq", None),
        P("dp", "seq", None),
        P("dp", None, "seq"),
        P("dp", None, "seq"),
        P("dp", None, None),
    )
    return jax.shard_map(
        local,
        mesh=mesh,
        in_specs=placed,
        out_specs=(P(None, "seq"), P("dp", "seq", None), P("dp", "seq", None)),
        check_vma=False,
    )
```

```python
import jax
import jax.numpy as jnp
from jax import lax
from jax.experimental import pallas as pl
from jax.experimental.pallas import tpu as pltpu
from jax.sharding import PartitionSpec as P

HEADS = 16
DIM = 128
LATENTS = 128
HALF = DIM // 2
SCALE = DIM ** (-0.5)
LOG2E = 1.4426950408889634
SIDE = 4
CHIPS = SIDE * SIDE
DEPTH = 8
ROWS = 2 * HALF + 16
MESH = pl.DeviceIdType.MESH
BF16 = jnp.bfloat16
F32 = jnp.float32

SENDS = (
    (3, 0), (1, 0), (0, 3), (0, 1), (3, 1), (1, 3), (3, 3), (1, 1),
    (2, 0), (0, 2), (2, 3), (2, 1), (3, 2), (1, 2), (2, 2),
)
MEETS = ((0, 0), (0, 1), (1, 0), (3, 0), (1, 1), (3, 1), (2, 0), (2, 1))
WORD = sum((dx + SIDE * row) << (4 * at) for at, (dx, row) in enumerate(MEETS))
STEPS = len(MEETS)
PIECES = 4


def matmul(a, b, a_dim, b_dim):
    return lax.dot_general(
        a, b, (((a_dim,), (b_dim,)), ((), ())), preferred_element_type=F32
    )


def kernel(
    latents, keys, values, out_grad, out_saved, log_norm,
    share, key_grad, value_grad,
    kb, vb, saved, norms, mine, pack, terms, parts, reduce_in, z_in, key_stage, value_stage,
    local_sem, token_sem, token_send, token_recv, pack_send, pack_recv,
    back_send, back_recv, reduce_send, reduce_recv, z_send, z_recv,
):
    z = lax.axis_index("dp")
    seat = lax.axis_index("seq")
    core = seat % 2
    chip = seat // 2
    x, y = chip // SIDE, chip % SIDE
    parity = chip % 2
    other = (z, chip * 2 + (1 - core))

    def head_at(step, of_core):
        code = lax.shift_right_logical(jnp.int32(WORD), jnp.int32(step) * 4) % 8
        row = (y // 2 + code // SIDE) % 2
        return ((x + SIDE - code % SIDE) % SIDE) * SIDE + of_core + 2 * row

    def ahead(dx, dy):
        return ((x + dx) % SIDE) * SIDE + (y + dy) % SIDE

    def columns_of(head):
        return pl.ds(pl.multiple_of(head * DIM, DIM), DIM)

    def tokens_in(step):
        head = head_at(step, core)
        cut = columns_of(head)
        at = head // 2
        return (
            pltpu.make_async_copy(keys.at[:, cut], kb.at[0, at], token_sem.at[0, at]),
            pltpu.make_async_copy(values.at[:, cut], vb.at[0, at], token_sem.at[1, at]),
        )

    def tokens_over(step):
        head = head_at(step, 1 - core)
        cut = columns_of(head)
        at = head // 2
        return tuple(
            pltpu.make_async_remote_copy(
                src_ref=source.at[:, cut], dst_ref=target.at[1, at],
                send_sem=token_send.at[n, at], recv_sem=token_recv.at[n, at],
                device_id=other, device_id_type=MESH,
            )
            for n, (source, target) in enumerate(((keys, kb), (values, vb)))
        )

    small = [
        pltpu.make_async_copy(latents, mine.at[pl.ds(0, HALF)], local_sem.at[0]),
        pltpu.make_async_copy(out_grad, mine.at[pl.ds(HALF, HALF)], local_sem.at[1]),
        pltpu.make_async_copy(out_saved, saved, local_sem.at[2]),
        pltpu.make_async_copy(log_norm, norms, local_sem.at[3]),
    ]
    for copy in small:
        copy.start()

    barrier = pltpu.get_barrier_semaphore()
    for dx in range(SIDE):
        for dy in range(SIDE):
            for flip in range(2):
                if dx or dy or flip:
                    to = (z, ahead(dx, dy) * 2 + (core + flip) % 2)
                    pl.semaphore_signal(barrier, inc=1, device_id=to, device_id_type=MESH)
    for dz in range(1, DEPTH):
        pl.semaphore_signal(barrier, inc=1, device_id=((z + dz) % DEPTH, seat), device_id_type=MESH)

    for step in range(STEPS):
        for copy in tokens_in(step):
            copy.start()

    for copy in small:
        copy.wait()
    grads = mine[HALF : 2 * HALF, :].astype(F32)
    dots = jnp.sum(grads * saved[...].astype(F32), axis=0, keepdims=True)
    top = dots.astype(BF16).astype(F32)
    middle = (dots - top).astype(BF16).astype(F32)
    rest = dots - top - middle
    row = lax.broadcasted_iota(jnp.int32, (16, DIM), 0)
    rows = jnp.where(row == 0, top, jnp.where(row == 1, middle, jnp.where(row == 2, rest, 0.0)))
    mine[2 * HALF : ROWS, :] = rows.astype(BF16)

    pl.semaphore_wait(barrier, 2 * CHIPS - 1 + DEPTH - 1)

    def give(to):
        return pltpu.make_async_remote_copy(
            src_ref=mine, dst_ref=pack.at[chip // 2, core],
            send_sem=pack_send.at[to], recv_sem=pack_recv.at[chip // 2, core],
            device_id=(z, to * 2 + parity), device_id_type=MESH,
        )

    def given(at, half):
        return pltpu.make_async_remote_copy(
            src_ref=mine, dst_ref=pack.at[at, half],
            send_sem=pack_send.at[at], recv_sem=pack_recv.at[at, half],
            device_id=other, device_id_type=MESH,
        )

    @pl.when(parity != core)
    def _():
        give(chip).start()

    for dx, dy in SENDS:
        give(ahead(dx, dy)).start()
    for step in range(STEPS):
        for copy in tokens_over(step):
            copy.start()

    @pl.when(parity == core)
    def _():
        keep = pltpu.make_async_copy(mine, pack.at[chip // 2, core], local_sem.at[4])
        keep.start()
        keep.wait()

    def reduce(head, half):
        at = head // 2
        return pltpu.make_async_remote_copy(
            src_ref=parts.at[at, half], dst_ref=reduce_in.at[chip],
            send_sem=reduce_send.at[at, half], recv_sem=reduce_recv.at[chip],
            device_id=(z, head * 2 + half), device_id_type=MESH,
        )

    def reduced(sender):
        return pltpu.make_async_remote_copy(
            src_ref=parts.at[0, 0], dst_ref=reduce_in.at[sender],
            send_sem=reduce_send.at[0, 0], recv_sem=reduce_recv.at[sender],
            device_id=other, device_id_type=MESH,
        )

    def back(head):
        cut = columns_of(head)
        at = head // 2
        return tuple(
            pltpu.make_async_remote_copy(
                src_ref=source.at[at], dst_ref=target.at[:, cut],
                send_sem=back_send.at[n, at], recv_sem=back_recv.at[n, at],
                device_id=other, device_id_type=MESH,
            )
            for n, (source, target) in enumerate(
                ((key_stage, key_grad), (value_stage, value_grad))
            )
        )

    def meet(step, carry):
        head = head_at(step, core)
        at = head // 2
        for half in range(2):
            @pl.when((head != chip) | (core != half))
            def _():
                given(at, half).wait_recv()

        query = jnp.concatenate([pack[at, 0, :HALF, :], pack[at, 1, :HALF, :]], axis=0)
        grad = jnp.concatenate(
            [pack[at, 0, HALF : 2 * HALF, :], pack[at, 1, HALF : 2 * HALF, :]], axis=0
        )
        dot_rows = pack[at, 0, 2 * HALF : ROWS, :].astype(F32)
        dot_rows += pack[at, 1, 2 * HALF : ROWS, :].astype(F32)
        row_dots = jnp.sum(dot_rows, axis=0, keepdims=True)
        norm = norms[pl.ds(head, 1), :] * LOG2E

        def scored(side):
            key = kb[side, at]
            scores = matmul(key, query, 1, 0)
            weight_grad = matmul(vb[side, at], grad, 1, 0)
            weights = jnp.exp2(scores * (SCALE * LOG2E) - norm)
            score_low = ((SCALE * weights) * (weight_grad - row_dots)).astype(BF16)
            return weights.astype(BF16), score_low, matmul(key, score_low, 0, 0)

        for copy in tokens_in(step):
            copy.wait()
        weights_low, score_low, term = scored(0)
        terms[...] = term
        cut = columns_of(head)
        value_grad[:, cut] = matmul(weights_low, grad, 1, 1).astype(BF16)
        key_grad[:, cut] = matmul(score_low, query, 1, 1).astype(BF16)

        for copy in tokens_over(step):
            copy.wait_recv()
        weights_low, score_low, term = scored(1)
        term += terms[...]
        parts[at, 0] = term[:HALF]
        parts[at, 1] = term[HALF:]
        for half in range(2):
            @pl.when((head != chip) | (core != half))
            def _():
                reduce(head, half).start()

        value_stage[at] = matmul(weights_low, grad, 1, 1).astype(BF16)
        key_stage[at] = matmul(score_low, query, 1, 1).astype(BF16)
        for copy in back(head):
            copy.start()
        return carry

    lax.fori_loop(0, STEPS, meet, 0)

    @pl.when(parity == core)
    def _():
        reduce_in[chip] = parts[chip // 2, core]

    @pl.when(parity != core)
    def _():
        reduced(chip).wait_recv()

    total = reduce_in[chip]
    for dx, dy in SENDS:
        sender = ahead(dx, dy)
        reduced(sender).wait_recv()
        total += reduce_in[sender]
    z_in[z] = total

    def cross(to):
        return pltpu.make_async_remote_copy(
            src_ref=z_in.at[z], dst_ref=z_in.at[z],
            send_sem=z_send.at[to], recv_sem=z_recv.at[z],
            device_id=(to, seat), device_id_type=MESH,
        )

    def crossed(sender):
        return pltpu.make_async_remote_copy(
            src_ref=z_in.at[z], dst_ref=z_in.at[sender],
            send_sem=z_send.at[sender], recv_sem=z_recv.at[sender],
            device_id=(sender, seat), device_id_type=MESH,
        )

    for dz in (4, 3, 5, 2, 6, 1, 7):
        cross((z + dz) % DEPTH).start()

    for step in range(STEPS):
        for copy in tokens_over(step):
            copy.wait_send()
        for copy in back(head_at(step, core)):
            copy.wait_send()
        for copy in back(head_at(step, 1 - core)):
            copy.wait_recv()
        head = head_at(step, core)
        for half in range(2):
            @pl.when((head != chip) | (core != half))
            def _():
                reduce(head, half).wait_send()
    for dx, dy in SENDS:
        give(ahead(dx, dy)).wait_send()

    @pl.when(parity != core)
    def _():
        give(chip).wait_send()

    for dz in (1, 7, 2, 6, 3, 5, 4):
        crossed((z + dz) % DEPTH).wait_recv()
    result = z_in[0]
    for at in range(1, DEPTH):
        result += z_in[at]
    share[...] = result
    for dz in range(1, DEPTH):
        cross((z + dz) % DEPTH).wait_send()


def finish(share, key_grad, value_grad, share_out, key_out, value_out, sem):
    copies = [pltpu.make_async_copy(share, share_out, sem.at[0])]
    rows = key_grad.shape[0] // PIECES
    for n, (source, target) in enumerate(((key_grad, key_out), (value_grad, value_out))):
        for at in range(PIECES):
            piece = pl.ds(at * rows, rows)
            copies.append(
                pltpu.make_async_copy(source.at[piece], target.at[piece], sem.at[1 + n * PIECES + at])
            )
    for copy in copies:
        copy.start()
    for copy in copies:
        copy.wait()


def local(latents, saved_keys, saved_values, out_grad, out_saved, log_norm):
    tokens, width = saved_keys.shape[1:]
    dma = pltpu.SemaphoreType.DMA
    hbm = pl.BlockSpec(memory_space=pltpu.MemorySpace.HBM)
    vmem = pl.BlockSpec(memory_space=pltpu.MemorySpace.VMEM)
    held = [
        pltpu.with_memory_space_constraint(a, pltpu.MemorySpace.HBM)
        for a in (
            latents.T, saved_keys[0], saved_values[0], out_grad[0].T, out_saved[0].T, log_norm[0]
        )
    ]
    share, key_grad, value_grad = pl.pallas_call(
        kernel,
        name="resampler_backward",
        out_shape=(
            jax.ShapeDtypeStruct((HALF, LATENTS), F32),
            jax.ShapeDtypeStruct((tokens, width), BF16),
            jax.ShapeDtypeStruct((tokens, width), BF16),
        ),
        in_specs=[hbm] * 6,
        out_specs=(vmem, vmem, vmem),
        scratch_shapes=[
            pltpu.VMEM((2, STEPS, tokens, DIM), BF16),
            pltpu.VMEM((2, STEPS, tokens, DIM), BF16),
            pltpu.VMEM((HALF, LATENTS), BF16),
            pltpu.VMEM((HEADS, LATENTS), F32),
            pltpu.VMEM((ROWS, LATENTS), BF16),
            pltpu.VMEM((STEPS, 2, ROWS, LATENTS), BF16),
            pltpu.VMEM((DIM, LATENTS), F32),
            pltpu.VMEM((STEPS, 2, HALF, LATENTS), F32),
            pltpu.VMEM((CHIPS, HALF, LATENTS), F32),
            pltpu.VMEM((DEPTH, HALF, LATENTS), F32),
            pltpu.VMEM((STEPS, tokens, DIM), BF16),
            pltpu.VMEM((STEPS, tokens, DIM), BF16),
            dma((5,)),
            dma((2, STEPS)), dma((2, STEPS)), dma((2, STEPS)),
            dma((CHIPS,)), dma((STEPS, 2)),
            dma((2, STEPS)), dma((2, STEPS)),
            dma((STEPS, 2)), dma((CHIPS,)),
            dma((DEPTH,)), dma((DEPTH,)),
        ],
        compiler_params=pltpu.CompilerParams(
            collective_id=0, has_side_effects=True, vmem_limit_bytes=40 << 20
        ),
    )(*held)
    share, key_grad, value_grad = pl.pallas_call(
        finish,
        name="results_out",
        out_shape=(
            jax.ShapeDtypeStruct((HALF, LATENTS), F32),
            jax.ShapeDtypeStruct((tokens, width), BF16),
            jax.ShapeDtypeStruct((tokens, width), BF16),
        ),
        in_specs=[vmem] * 3,
        out_specs=(hbm, hbm, hbm),
        scratch_shapes=[dma((1 + 2 * PIECES,))],
        compiler_params=pltpu.CompilerParams(vmem_limit_bytes=1 << 20),
    )(share, key_grad, value_grad)
    return share.T, key_grad[None], value_grad[None]


def solution(mesh):
    placed = (
        P(None, "seq"),
        P("dp", "seq", None),
        P("dp", "seq", None),
        P("dp", None, "seq"),
        P("dp", None, "seq"),
        P("dp", None, None),
    )
    return jax.shard_map(
        local,
        mesh=mesh,
        in_specs=placed,
        out_specs=(P(None, "seq"), P("dp", "seq", None), P("dp", "seq", None)),
        check_vma=False,
    )
```

```python
import jax
import jax.numpy as jnp
from jax import lax
from jax.experimental import pallas as pl
from jax.experimental.pallas import tpu as pltpu
from jax.sharding import PartitionSpec as P

HEADS = 16
DIM = 128
LATENTS = 128
HALF = DIM // 2
SCALE = DIM ** (-0.5)
LOG2E = 1.4426950408889634
SIDE = 4
CHIPS = SIDE * SIDE
DEPTH = 8
ROWS = 2 * HALF + 8
MESH = pl.DeviceIdType.MESH
BF16 = jnp.bfloat16
F32 = jnp.float32

SENDS = (
    (3, 0), (1, 0), (0, 3), (0, 1), (3, 1), (1, 3), (3, 3), (1, 1),
    (2, 0), (0, 2), (2, 3), (2, 1), (3, 2), (1, 2), (2, 2),
)
MEETS = ((0, 0), (0, 1), (1, 0), (3, 0), (1, 1), (3, 1), (2, 0), (2, 1))
WORD = sum((dx + SIDE * row) << (4 * at) for at, (dx, row) in enumerate(MEETS))
STEPS = len(MEETS)
PIECES = 4
BASE, DIGITS = 16, 2
CODED = HALF + HALF // DIGITS


def matmul(a, b, a_dim, b_dim):
    return lax.dot_general(
        a, b, (((a_dim,), (b_dim,)), ((), ())), preferred_element_type=F32
    )


def coded(a):
    high = a.astype(BF16)
    near = high.astype(F32)
    over = jnp.where(near == 0.0, 1.0, near)
    digit = jnp.floor(((a - near) / over) * (128.0 * BASE) + 0.5 * BASE)
    digit = jnp.clip(digit, 0.0, BASE - 1.0)
    step = HALF // DIGITS
    low = digit[:step]
    for at in range(step, HALF, step):
        low = low * BASE + digit[at : at + step]
    return high, (low - 128.0).astype(BF16)


def decoded(ref):
    near = ref[:HALF, :].astype(F32)
    low = ref[HALF:CODED, :].astype(F32) + 128.0
    digits = []
    for _ in range(DIGITS - 1):
        rest = jnp.floor(low * (1.0 / BASE))
        digits.append(low - rest * BASE)
        low = rest
    digit = jnp.concatenate([low] + digits[::-1], axis=0)
    return near + near * ((digit + (0.5 - 0.5 * BASE)) * (1.0 / (128.0 * BASE)))


def store_coded(ref, a):
    high, low = coded(a)
    ref[:HALF, :] = high
    ref[HALF:CODED, :] = low


def kernel(
    latents, keys, values, out_grad, out_saved, log_norm,
    share, key_grad, value_grad,
    kb, vb, saved, norms, mine, pack, terms, parts, reduce_in, z_in, key_stage, value_stage,
    local_sem, token_sem, token_send, token_recv, pack_send, pack_recv,
    back_send, back_recv, reduce_send, reduce_recv, z_send, z_recv,
):
    z = lax.axis_index("dp")
    seat = lax.axis_index("seq")
    core = seat % 2
    chip = seat // 2
    x, y = chip // SIDE, chip % SIDE
    parity = chip % 2
    other = (z, chip * 2 + (1 - core))

    def head_at(step, of_core):
        code = lax.shift_right_logical(jnp.int32(WORD), jnp.int32(step) * 4) % 8
        row = (y // 2 + code // SIDE) % 2
        return ((x + SIDE - code % SIDE) % SIDE) * SIDE + of_core + 2 * row

    def ahead(dx, dy):
        return ((x + dx) % SIDE) * SIDE + (y + dy) % SIDE

    def columns_of(head):
        return pl.ds(pl.multiple_of(head * DIM, DIM), DIM)

    def tokens_in(step):
        head = head_at(step, core)
        cut = columns_of(head)
        at = head // 2
        return (
            pltpu.make_async_copy(keys.at[:, cut], kb.at[0, at], token_sem.at[0, at]),
            pltpu.make_async_copy(values.at[:, cut], vb.at[0, at], token_sem.at[1, at]),
        )

    def tokens_over(step):
        head = head_at(step, 1 - core)
        cut = columns_of(head)
        at = head // 2
        return tuple(
            pltpu.make_async_remote_copy(
                src_ref=source.at[:, cut], dst_ref=target.at[1, at],
                send_sem=token_send.at[n, at], recv_sem=token_recv.at[n, at],
                device_id=other, device_id_type=MESH,
            )
            for n, (source, target) in enumerate(((keys, kb), (values, vb)))
        )

    small = [
        pltpu.make_async_copy(latents, mine.at[pl.ds(0, HALF)], local_sem.at[0]),
        pltpu.make_async_copy(out_grad, mine.at[pl.ds(HALF, HALF)], local_sem.at[1]),
        pltpu.make_async_copy(out_saved, saved, local_sem.at[2]),
        pltpu.make_async_copy(log_norm, norms, local_sem.at[3]),
    ]
    for copy in small:
        copy.start()

    barrier = pltpu.get_barrier_semaphore()
    for dx in range(SIDE):
        for dy in range(SIDE):
            for flip in range(2):
                if dx or dy or flip:
                    to = (z, ahead(dx, dy) * 2 + (core + flip) % 2)
                    pl.semaphore_signal(barrier, inc=1, device_id=to, device_id_type=MESH)
    for dz in range(1, DEPTH):
        pl.semaphore_signal(barrier, inc=1, device_id=((z + dz) % DEPTH, seat), device_id_type=MESH)

    for step in range(STEPS):
        for copy in tokens_in(step):
            copy.start()

    for copy in small:
        copy.wait()
    grads = mine[HALF : 2 * HALF, :].astype(F32)
    dots = jnp.sum(grads * saved[...].astype(F32), axis=0, keepdims=True)
    top = dots.astype(BF16).astype(F32)
    middle = (dots - top).astype(BF16).astype(F32)
    rest = dots - top - middle
    row = lax.broadcasted_iota(jnp.int32, (8, DIM), 0)
    rows = jnp.where(row == 0, top, jnp.where(row == 1, middle, jnp.where(row == 2, rest, 0.0)))
    mine[2 * HALF : ROWS, :] = rows.astype(BF16)

    pl.semaphore_wait(barrier, 2 * CHIPS - 1 + DEPTH - 1)

    def give(to):
        return pltpu.make_async_remote_copy(
            src_ref=mine, dst_ref=pack.at[chip // 2, core],
            send_sem=pack_send.at[to], recv_sem=pack_recv.at[chip // 2, core],
            device_id=(z, to * 2 + parity), device_id_type=MESH,
        )

    def given(at, half):
        return pltpu.make_async_remote_copy(
            src_ref=mine, dst_ref=pack.at[at, half],
            send_sem=pack_send.at[at], recv_sem=pack_recv.at[at, half],
            device_id=other, device_id_type=MESH,
        )

    @pl.when(parity != core)
    def _():
        give(chip).start()

    for dx, dy in SENDS:
        give(ahead(dx, dy)).start()
    for step in range(STEPS):
        for copy in tokens_over(step):
            copy.start()

    @pl.when(parity == core)
    def _():
        keep = pltpu.make_async_copy(mine, pack.at[chip // 2, core], local_sem.at[4])
        keep.start()
        keep.wait()

    def reduce(head, half):
        at = head // 2
        return pltpu.make_async_remote_copy(
            src_ref=parts.at[at, half], dst_ref=reduce_in.at[chip],
            send_sem=reduce_send.at[at, half], recv_sem=reduce_recv.at[chip],
            device_id=(z, head * 2 + half), device_id_type=MESH,
        )

    def reduced(sender):
        return pltpu.make_async_remote_copy(
            src_ref=parts.at[0, 0], dst_ref=reduce_in.at[sender],
            send_sem=reduce_send.at[0, 0], recv_sem=reduce_recv.at[sender],
            device_id=other, device_id_type=MESH,
        )

    def back(head):
        cut = columns_of(head)
        at = head // 2
        return tuple(
            pltpu.make_async_remote_copy(
                src_ref=source.at[at], dst_ref=target.at[:, cut],
                send_sem=back_send.at[n, at], recv_sem=back_recv.at[n, at],
                device_id=other, device_id_type=MESH,
            )
            for n, (source, target) in enumerate(
                ((key_stage, key_grad), (value_stage, value_grad))
            )
        )

    def meet(step, carry):
        head = head_at(step, core)
        at = head // 2
        for half in range(2):
            @pl.when((head != chip) | (core != half))
            def _():
                given(at, half).wait_recv()

        query = jnp.concatenate([pack[at, 0, :HALF, :], pack[at, 1, :HALF, :]], axis=0)
        grad = jnp.concatenate(
            [pack[at, 0, HALF : 2 * HALF, :], pack[at, 1, HALF : 2 * HALF, :]], axis=0
        )
        dot_rows = pack[at, 0, 2 * HALF : ROWS, :].astype(F32)
        dot_rows += pack[at, 1, 2 * HALF : ROWS, :].astype(F32)
        row_dots = jnp.sum(dot_rows, axis=0, keepdims=True)
        norm = norms[pl.ds(head, 1), :] * LOG2E

        def scored(side):
            key = kb[side, at]
            scores = matmul(key, query, 1, 0)
            weight_grad = matmul(vb[side, at], grad, 1, 0)
            weights = jnp.exp2(scores * (SCALE * LOG2E) - norm)
            score_low = ((SCALE * weights) * (weight_grad - row_dots)).astype(BF16)
            return weights.astype(BF16), score_low, matmul(key, score_low, 0, 0)

        for copy in tokens_in(step):
            copy.wait()
        weights_low, score_low, term = scored(0)
        terms[...] = term
        cut = columns_of(head)
        value_grad[:, cut] = matmul(weights_low, grad, 1, 1).astype(BF16)
        key_grad[:, cut] = matmul(score_low, query, 1, 1).astype(BF16)

        for copy in tokens_over(step):
            copy.wait_recv()
        weights_low, score_low, term = scored(1)
        term += terms[...]
        store_coded(parts.at[at, 0], term[:HALF])
        store_coded(parts.at[at, 1], term[HALF:])
        for half in range(2):
            @pl.when((head != chip) | (core != half))
            def _():
                reduce(head, half).start()

        value_stage[at] = matmul(weights_low, grad, 1, 1).astype(BF16)
        key_stage[at] = matmul(score_low, query, 1, 1).astype(BF16)
        for copy in back(head):
            copy.start()
        return carry

    lax.fori_loop(0, STEPS, meet, 0)

    @pl.when(parity == core)
    def _():
        reduce_in[chip] = parts[chip // 2, core]

    @pl.when(parity != core)
    def _():
        reduced(chip).wait_recv()

    total = decoded(reduce_in.at[chip])
    for dx, dy in SENDS:
        sender = ahead(dx, dy)
        reduced(sender).wait_recv()
        total += decoded(reduce_in.at[sender])
    store_coded(z_in.at[z], total)

    def cross(to):
        return pltpu.make_async_remote_copy(
            src_ref=z_in.at[z], dst_ref=z_in.at[z],
            send_sem=z_send.at[to], recv_sem=z_recv.at[z],
            device_id=(to, seat), device_id_type=MESH,
        )

    def crossed(sender):
        return pltpu.make_async_remote_copy(
            src_ref=z_in.at[z], dst_ref=z_in.at[sender],
            send_sem=z_send.at[sender], recv_sem=z_recv.at[sender],
            device_id=(sender, seat), device_id_type=MESH,
        )

    for dz in (4, 3, 5, 2, 6, 1, 7):
        cross((z + dz) % DEPTH).start()

    for step in range(STEPS):
        for copy in tokens_over(step):
            copy.wait_send()
        for copy in back(head_at(step, core)):
            copy.wait_send()
        for copy in back(head_at(step, 1 - core)):
            copy.wait_recv()
        head = head_at(step, core)
        for half in range(2):
            @pl.when((head != chip) | (core != half))
            def _():
                reduce(head, half).wait_send()
    for dx, dy in SENDS:
        give(ahead(dx, dy)).wait_send()

    @pl.when(parity != core)
    def _():
        give(chip).wait_send()

    for dz in (1, 7, 2, 6, 3, 5, 4):
        crossed((z + dz) % DEPTH).wait_recv()
    result = decoded(z_in.at[0])
    for at in range(1, DEPTH):
        result += decoded(z_in.at[at])
    share[...] = result
    for dz in range(1, DEPTH):
        cross((z + dz) % DEPTH).wait_send()


def finish(share, key_grad, value_grad, share_out, key_out, value_out, sem):
    copies = [pltpu.make_async_copy(share, share_out, sem.at[0])]
    rows = key_grad.shape[0] // PIECES
    for n, (source, target) in enumerate(((key_grad, key_out), (value_grad, value_out))):
        for at in range(PIECES):
            piece = pl.ds(at * rows, rows)
            copies.append(
                pltpu.make_async_copy(source.at[piece], target.at[piece], sem.at[1 + n * PIECES + at])
            )
    for copy in copies:
        copy.start()
    for copy in copies:
        copy.wait()


def local(latents, saved_keys, saved_values, out_grad, out_saved, log_norm):
    tokens, width = saved_keys.shape[1:]
    dma = pltpu.SemaphoreType.DMA
    hbm = pl.BlockSpec(memory_space=pltpu.MemorySpace.HBM)
    vmem = pl.BlockSpec(memory_space=pltpu.MemorySpace.VMEM)
    held = [
        pltpu.with_memory_space_constraint(a, pltpu.MemorySpace.HBM)
        for a in (
            latents.T, saved_keys[0], saved_values[0], out_grad[0].T, out_saved[0].T, log_norm[0]
        )
    ]
    share, key_grad, value_grad = pl.pallas_call(
        kernel,
        name="resampler_backward",
        out_shape=(
            jax.ShapeDtypeStruct((HALF, LATENTS), F32),
            jax.ShapeDtypeStruct((tokens, width), BF16),
            jax.ShapeDtypeStruct((tokens, width), BF16),
        ),
        in_specs=[hbm] * 6,
        out_specs=(vmem, vmem, vmem),
        scratch_shapes=[
            pltpu.VMEM((2, STEPS, tokens, DIM), BF16),
            pltpu.VMEM((2, STEPS, tokens, DIM), BF16),
            pltpu.VMEM((HALF, LATENTS), BF16),
            pltpu.VMEM((HEADS, LATENTS), F32),
            pltpu.VMEM((ROWS, LATENTS), BF16),
            pltpu.VMEM((STEPS, 2, ROWS, LATENTS), BF16),
            pltpu.VMEM((DIM, LATENTS), F32),
            pltpu.VMEM((STEPS, 2, CODED, LATENTS), BF16),
            pltpu.VMEM((CHIPS, CODED, LATENTS), BF16),
            pltpu.VMEM((DEPTH, CODED, LATENTS), BF16),
            pltpu.VMEM((STEPS, tokens, DIM), BF16),
            pltpu.VMEM((STEPS, tokens, DIM), BF16),
            dma((5,)),
            dma((2, STEPS)), dma((2, STEPS)), dma((2, STEPS)),
            dma((CHIPS,)), dma((STEPS, 2)),
            dma((2, STEPS)), dma((2, STEPS)),
            dma((STEPS, 2)), dma((CHIPS,)),
            dma((DEPTH,)), dma((DEPTH,)),
        ],
        compiler_params=pltpu.CompilerParams(
            collective_id=0, has_side_effects=True, vmem_limit_bytes=40 << 20
        ),
    )(*held)
    share, key_grad, value_grad = pl.pallas_call(
        finish,
        name="results_out",
        out_shape=(
            jax.ShapeDtypeStruct((HALF, LATENTS), F32),
            jax.ShapeDtypeStruct((tokens, width), BF16),
            jax.ShapeDtypeStruct((tokens, width), BF16),
        ),
        in_specs=[vmem] * 3,
        out_specs=(hbm, hbm, hbm),
        scratch_shapes=[dma((1 + 2 * PIECES,))],
        compiler_params=pltpu.CompilerParams(vmem_limit_bytes=1 << 20),
    )(share, key_grad, value_grad)
    return share.T, key_grad[None], value_grad[None]


def solution(mesh):
    placed = (
        P(None, "seq"),
        P("dp", "seq", None),
        P("dp", "seq", None),
        P("dp", None, "seq"),
        P("dp", None, "seq"),
        P("dp", None, None),
    )
    return jax.shard_map(
        local,
        mesh=mesh,
        in_specs=placed,
        out_specs=(P(None, "seq"), P("dp", "seq", None), P("dp", "seq", None)),
        check_vma=False,
    )
```

```python
import jax
import jax.numpy as jnp
from jax import lax
from jax.experimental import pallas as pl
from jax.experimental.pallas import tpu as pltpu
from jax.sharding import PartitionSpec as P

HEADS = 16
DIM = 128
LATENTS = 128
HALF = DIM // 2
SCALE = DIM ** (-0.5)
LOG2E = 1.4426950408889634
SIDE = 4
CHIPS = SIDE * SIDE
DEPTH = 8
ROWS = 2 * HALF + 8
MESH = pl.DeviceIdType.MESH
BF16 = jnp.bfloat16
F32 = jnp.float32

SENDS = (
    (3, 0), (1, 0), (0, 3), (0, 1), (3, 1), (1, 3), (3, 3), (1, 1),
    (2, 0), (0, 2), (2, 3), (2, 1), (3, 2), (1, 2), (2, 2),
)
MEETS = ((0, 0), (0, 1), (1, 0), (3, 0), (1, 1), (3, 1), (2, 0), (2, 1))
WORD = sum((dx + SIDE * row) << (4 * at) for at, (dx, row) in enumerate(MEETS))
STEPS = len(MEETS)
PIECES = 4
EARLY = 6
BASE, DIGITS = 4, 4
CODED = HALF + HALF // DIGITS


def matmul(a, b, a_dim, b_dim):
    return lax.dot_general(
        a, b, (((a_dim,), (b_dim,)), ((), ())), preferred_element_type=F32
    )


def coded(a):
    high = a.astype(BF16)
    near = high.astype(F32)
    over = jnp.where(near == 0.0, 1.0, near)
    digit = jnp.floor(((a - near) / over) * (128.0 * BASE) + 0.5 * BASE)
    digit = jnp.clip(digit, 0.0, BASE - 1.0)
    step = HALF // DIGITS
    low = digit[:step]
    for at in range(step, HALF, step):
        low = low * BASE + digit[at : at + step]
    return high, (low - 128.0).astype(BF16)


def decoded(ref):
    near = ref[:HALF, :].astype(F32)
    low = ref[HALF:CODED, :].astype(F32) + 128.0
    digits = []
    for _ in range(DIGITS - 1):
        rest = jnp.floor(low * (1.0 / BASE))
        digits.append(low - rest * BASE)
        low = rest
    digit = jnp.concatenate([low] + digits[::-1], axis=0)
    return near + near * ((digit + (0.5 - 0.5 * BASE)) * (1.0 / (128.0 * BASE)))


def store_coded(ref, a):
    high, low = coded(a)
    ref[:HALF, :] = high
    ref[HALF:CODED, :] = low


def kernel(
    latents, keys, values, out_grad, out_saved, log_norm,
    share, key_grad, value_grad,
    kb, vb, saved, norms, mine, pack, terms, parts, reduce_in, z_in, key_stage, value_stage, weights_held, score_held,
    local_sem, token_sem, token_send, token_recv, pack_send, pack_recv,
    back_send, back_recv, reduce_send, reduce_recv, z_send, z_recv,
):
    z = lax.axis_index("dp")
    seat = lax.axis_index("seq")
    core = seat % 2
    chip = seat // 2
    x, y = chip // SIDE, chip % SIDE
    parity = chip % 2
    other = (z, chip * 2 + (1 - core))

    def head_at(step, of_core):
        code = lax.shift_right_logical(jnp.int32(WORD), jnp.int32(step) * 4) % 8
        row = (y // 2 + code // SIDE) % 2
        return ((x + SIDE - code % SIDE) % SIDE) * SIDE + of_core + 2 * row

    def ahead(dx, dy):
        return ((x + dx) % SIDE) * SIDE + (y + dy) % SIDE

    def columns_of(head):
        return pl.ds(pl.multiple_of(head * DIM, DIM), DIM)

    def tokens_in(step):
        head = head_at(step, core)
        cut = columns_of(head)
        at = head // 2
        return (
            pltpu.make_async_copy(keys.at[:, cut], kb.at[0, at], token_sem.at[0, at]),
            pltpu.make_async_copy(values.at[:, cut], vb.at[0, at], token_sem.at[1, at]),
        )

    def tokens_over(step):
        head = head_at(step, 1 - core)
        cut = columns_of(head)
        at = head // 2
        return tuple(
            pltpu.make_async_remote_copy(
                src_ref=source.at[:, cut], dst_ref=target.at[1, at],
                send_sem=token_send.at[n, at], recv_sem=token_recv.at[n, at],
                device_id=other, device_id_type=MESH,
            )
            for n, (source, target) in enumerate(((keys, kb), (values, vb)))
        )

    small = [
        pltpu.make_async_copy(latents, mine.at[pl.ds(0, HALF)], local_sem.at[0]),
        pltpu.make_async_copy(out_grad, mine.at[pl.ds(HALF, HALF)], local_sem.at[1]),
        pltpu.make_async_copy(out_saved, saved, local_sem.at[2]),
        pltpu.make_async_copy(log_norm, norms, local_sem.at[3]),
    ]
    for copy in small:
        copy.start()

    barrier = pltpu.get_barrier_semaphore()
    for dx in range(SIDE):
        for dy in range(SIDE):
            for flip in range(2):
                if dx or dy or flip:
                    to = (z, ahead(dx, dy) * 2 + (core + flip) % 2)
                    pl.semaphore_signal(barrier, inc=1, device_id=to, device_id_type=MESH)
    for dz in range(1, DEPTH):
        pl.semaphore_signal(barrier, inc=1, device_id=((z + dz) % DEPTH, seat), device_id_type=MESH)

    for step in range(STEPS):
        for copy in tokens_in(step):
            copy.start()

    for copy in small:
        copy.wait()
    grads = mine[HALF : 2 * HALF, :].astype(F32)
    dots = jnp.sum(grads * saved[...].astype(F32), axis=0, keepdims=True)
    top = dots.astype(BF16).astype(F32)
    middle = (dots - top).astype(BF16).astype(F32)
    rest = dots - top - middle
    row = lax.broadcasted_iota(jnp.int32, (8, DIM), 0)
    rows = jnp.where(row == 0, top, jnp.where(row == 1, middle, jnp.where(row == 2, rest, 0.0)))
    mine[2 * HALF : ROWS, :] = rows.astype(BF16)

    pl.semaphore_wait(barrier, 2 * CHIPS - 1 + DEPTH - 1)

    def give(to):
        return pltpu.make_async_remote_copy(
            src_ref=mine, dst_ref=pack.at[chip // 2, core],
            send_sem=pack_send.at[to], recv_sem=pack_recv.at[chip // 2, core],
            device_id=(z, to * 2 + parity), device_id_type=MESH,
        )

    def given(at, half):
        return pltpu.make_async_remote_copy(
            src_ref=mine, dst_ref=pack.at[at, half],
            send_sem=pack_send.at[at], recv_sem=pack_recv.at[at, half],
            device_id=other, device_id_type=MESH,
        )

    @pl.when(parity != core)
    def _():
        give(chip).start()

    for dx, dy in SENDS:
        give(ahead(dx, dy)).start()
    for step in range(STEPS):
        for copy in tokens_over(step):
            copy.start()

    @pl.when(parity == core)
    def _():
        keep = pltpu.make_async_copy(mine, pack.at[chip // 2, core], local_sem.at[4])
        keep.start()
        keep.wait()

    def reduce(head, half):
        at = head // 2
        return pltpu.make_async_remote_copy(
            src_ref=parts.at[at, half], dst_ref=reduce_in.at[chip],
            send_sem=reduce_send.at[at, half], recv_sem=reduce_recv.at[chip],
            device_id=(z, head * 2 + half), device_id_type=MESH,
        )

    def reduced(sender):
        return pltpu.make_async_remote_copy(
            src_ref=parts.at[0, 0], dst_ref=reduce_in.at[sender],
            send_sem=reduce_send.at[0, 0], recv_sem=reduce_recv.at[sender],
            device_id=other, device_id_type=MESH,
        )

    def back(head):
        cut = columns_of(head)
        at = head // 2
        return tuple(
            pltpu.make_async_remote_copy(
                src_ref=source.at[at], dst_ref=target.at[:, cut],
                send_sem=back_send.at[n, at], recv_sem=back_recv.at[n, at],
                device_id=other, device_id_type=MESH,
            )
            for n, (source, target) in enumerate(
                ((key_stage, key_grad), (value_stage, value_grad))
            )
        )

    def both_halves(at):
        query = jnp.concatenate([pack[at, 0, :HALF, :], pack[at, 1, :HALF, :]], axis=0)
        grad = jnp.concatenate(
            [pack[at, 0, HALF : 2 * HALF, :], pack[at, 1, HALF : 2 * HALF, :]], axis=0
        )
        return query, grad

    def meet(step, carry):
        head = head_at(step, core)
        at = head // 2
        for half in range(2):
            @pl.when((head != chip) | (core != half))
            def _():
                given(at, half).wait_recv()

        query, grad = both_halves(at)
        dot_rows = pack[at, 0, 2 * HALF : ROWS, :].astype(F32)
        dot_rows += pack[at, 1, 2 * HALF : ROWS, :].astype(F32)
        row_dots = jnp.sum(dot_rows, axis=0, keepdims=True)
        norm = norms[pl.ds(head, 1), :] * LOG2E

        def scored(side):
            key = kb[side, at]
            scores = matmul(key, query, 1, 0)
            weight_grad = matmul(vb[side, at], grad, 1, 0)
            weights = jnp.exp2(scores * (SCALE * LOG2E) - norm)
            score_low = ((SCALE * weights) * (weight_grad - row_dots)).astype(BF16)
            return weights.astype(BF16), score_low, matmul(key, score_low, 0, 0)

        for copy in tokens_in(step):
            copy.wait()
        weights_low, score_low, term = scored(0)
        terms[...] = term
        weights_held[0, at] = weights_low
        score_held[0, at] = score_low

        for copy in tokens_over(step):
            copy.wait_recv()
        weights_low, score_low, term = scored(1)
        term += terms[...]
        store_coded(parts.at[at, 0], term[:HALF])
        store_coded(parts.at[at, 1], term[HALF:])
        for half in range(2):
            @pl.when((head != chip) | (core != half))
            def _():
                reduce(head, half).start()

        weights_held[1, at] = weights_low
        score_held[1, at] = score_low
        return carry

    def spread(step, carry):
        head = head_at(step, core)
        at = head // 2
        query, grad = both_halves(at)
        value_stage[at] = matmul(weights_held[1, at], grad, 1, 1).astype(BF16)
        key_stage[at] = matmul(score_held[1, at], query, 1, 1).astype(BF16)
        for copy in back(head):
            copy.start()
        cut = columns_of(head)
        value_grad[:, cut] = matmul(weights_held[0, at], grad, 1, 1).astype(BF16)
        key_grad[:, cut] = matmul(score_held[0, at], query, 1, 1).astype(BF16)
        return carry

    lax.fori_loop(0, STEPS, meet, 0)
    lax.fori_loop(0, EARLY, spread, 0)

    @pl.when(parity == core)
    def _():
        reduce_in[chip] = parts[chip // 2, core]

    @pl.when(parity != core)
    def _():
        reduced(chip).wait_recv()

    total = decoded(reduce_in.at[chip])
    for dx, dy in SENDS:
        sender = ahead(dx, dy)
        reduced(sender).wait_recv()
        total += decoded(reduce_in.at[sender])
    store_coded(z_in.at[z], total)

    def cross(to):
        return pltpu.make_async_remote_copy(
            src_ref=z_in.at[z], dst_ref=z_in.at[z],
            send_sem=z_send.at[to], recv_sem=z_recv.at[z],
            device_id=(to, seat), device_id_type=MESH,
        )

    def crossed(sender):
        return pltpu.make_async_remote_copy(
            src_ref=z_in.at[z], dst_ref=z_in.at[sender],
            send_sem=z_send.at[sender], recv_sem=z_recv.at[sender],
            device_id=(sender, seat), device_id_type=MESH,
        )

    for dz in (4, 3, 5, 2, 6, 1, 7):
        cross((z + dz) % DEPTH).start()
    lax.fori_loop(EARLY, STEPS, spread, 0)

    for step in range(STEPS):
        for copy in tokens_over(step):
            copy.wait_send()
        for copy in back(head_at(step, core)):
            copy.wait_send()
        for copy in back(head_at(step, 1 - core)):
            copy.wait_recv()
        head = head_at(step, core)
        for half in range(2):
            @pl.when((head != chip) | (core != half))
            def _():
                reduce(head, half).wait_send()
    for dx, dy in SENDS:
        give(ahead(dx, dy)).wait_send()

    @pl.when(parity != core)
    def _():
        give(chip).wait_send()

    for dz in (1, 7, 2, 6, 3, 5, 4):
        crossed((z + dz) % DEPTH).wait_recv()
    result = decoded(z_in.at[0])
    for at in range(1, DEPTH):
        result += decoded(z_in.at[at])
    share[...] = result
    for dz in range(1, DEPTH):
        cross((z + dz) % DEPTH).wait_send()


def finish(share, key_grad, value_grad, share_out, key_out, value_out, sem):
    copies = [pltpu.make_async_copy(share, share_out, sem.at[0])]
    rows = key_grad.shape[0] // PIECES
    for n, (source, target) in enumerate(((key_grad, key_out), (value_grad, value_out))):
        for at in range(PIECES):
            piece = pl.ds(at * rows, rows)
            copies.append(
                pltpu.make_async_copy(source.at[piece], target.at[piece], sem.at[1 + n * PIECES + at])
            )
    for copy in copies:
        copy.start()
    for copy in copies:
        copy.wait()


def local(latents, saved_keys, saved_values, out_grad, out_saved, log_norm):
    tokens, width = saved_keys.shape[1:]
    dma = pltpu.SemaphoreType.DMA
    hbm = pl.BlockSpec(memory_space=pltpu.MemorySpace.HBM)
    vmem = pl.BlockSpec(memory_space=pltpu.MemorySpace.VMEM)
    held = [
        pltpu.with_memory_space_constraint(a, pltpu.MemorySpace.HBM)
        for a in (
            latents.T, saved_keys[0], saved_values[0], out_grad[0].T, out_saved[0].T, log_norm[0]
        )
    ]
    share, key_grad, value_grad = pl.pallas_call(
        kernel,
        name="resampler_backward",
        out_shape=(
            jax.ShapeDtypeStruct((HALF, LATENTS), F32),
            jax.ShapeDtypeStruct((tokens, width), BF16),
            jax.ShapeDtypeStruct((tokens, width), BF16),
        ),
        in_specs=[hbm] * 6,
        out_specs=(vmem, vmem, vmem),
        scratch_shapes=[
            pltpu.VMEM((2, STEPS, tokens, DIM), BF16),
            pltpu.VMEM((2, STEPS, tokens, DIM), BF16),
            pltpu.VMEM((HALF, LATENTS), BF16),
            pltpu.VMEM((HEADS, LATENTS), F32),
            pltpu.VMEM((ROWS, LATENTS), BF16),
            pltpu.VMEM((STEPS, 2, ROWS, LATENTS), BF16),
            pltpu.VMEM((DIM, LATENTS), F32),
            pltpu.VMEM((STEPS, 2, CODED, LATENTS), BF16),
            pltpu.VMEM((CHIPS, CODED, LATENTS), BF16),
            pltpu.VMEM((DEPTH, CODED, LATENTS), BF16),
            pltpu.VMEM((STEPS, tokens, DIM), BF16),
            pltpu.VMEM((STEPS, tokens, DIM), BF16),
            pltpu.VMEM((2, STEPS, tokens, DIM), BF16),
            pltpu.VMEM((2, STEPS, tokens, DIM), BF16),
            dma((5,)),
            dma((2, STEPS)), dma((2, STEPS)), dma((2, STEPS)),
            dma((CHIPS,)), dma((STEPS, 2)),
            dma((2, STEPS)), dma((2, STEPS)),
            dma((STEPS, 2)), dma((CHIPS,)),
            dma((DEPTH,)), dma((DEPTH,)),
        ],
        compiler_params=pltpu.CompilerParams(
            collective_id=0, has_side_effects=True, vmem_limit_bytes=40 << 20
        ),
    )(*held)
    share, key_grad, value_grad = pl.pallas_call(
        finish,
        name="results_out",
        out_shape=(
            jax.ShapeDtypeStruct((HALF, LATENTS), F32),
            jax.ShapeDtypeStruct((tokens, width), BF16),
            jax.ShapeDtypeStruct((tokens, width), BF16),
        ),
        in_specs=[vmem] * 3,
        out_specs=(hbm, hbm, hbm),
        scratch_shapes=[dma((1 + 2 * PIECES,))],
        compiler_params=pltpu.CompilerParams(vmem_limit_bytes=1 << 20),
    )(share, key_grad, value_grad)
    return share.T, key_grad[None], value_grad[None]


def solution(mesh):
    placed = (
        P(None, "seq"),
        P("dp", "seq", None),
        P("dp", "seq", None),
        P("dp", None, "seq"),
        P("dp", None, "seq"),
        P("dp", None, None),
    )
    return jax.shard_map(
        local,
        mesh=mesh,
        in_specs=placed,
        out_specs=(P(None, "seq"), P("dp", "seq", None), P("dp", "seq", None)),
        check_vma=False,
    )
```

```python
import jax
import jax.numpy as jnp
from jax import lax
from jax.experimental import pallas as pl
from jax.experimental.pallas import tpu as pltpu
from jax.sharding import PartitionSpec as P

HEADS = 16
DIM = 128
LATENTS = 128
HALF = DIM // 2
SCALE = DIM ** (-0.5)
LOG2E = 1.4426950408889634
SIDE = 4
CHIPS = SIDE * SIDE
DEPTH = 8
ROWS = 2 * HALF + 8
MESH = pl.DeviceIdType.MESH
BF16 = jnp.bfloat16
F32 = jnp.float32

SENDS = (
    (3, 0), (1, 0), (0, 3), (0, 1), (3, 1), (1, 3), (3, 3), (1, 1),
    (2, 0), (0, 2), (2, 3), (2, 1), (3, 2), (1, 2), (2, 2),
)
MEETS = ((0, 0), (0, 1), (1, 0), (1, 1), (3, 1), (2, 0), (2, 1), (3, 0))
WORD = sum((dx + SIDE * row) << (4 * at) for at, (dx, row) in enumerate(MEETS))
STEPS = len(MEETS)
PIECES = 16
EARLY = 6
BASE, DIGITS = 4, 4
CODED = HALF + HALF // DIGITS


def matmul(a, b, a_dim, b_dim):
    return lax.dot_general(
        a, b, (((a_dim,), (b_dim,)), ((), ())), preferred_element_type=F32
    )


def power(near):
    size = jnp.maximum(jnp.abs(near), 1e-30)
    return jnp.exp2(jnp.floor(jnp.log2(size) + 0.002))


def coded(a):
    high = a.astype(BF16)
    near = high.astype(F32)
    digit = jnp.floor((a - near) * ((128.0 * BASE) / power(near)) + 0.5 * BASE)
    digit = jnp.clip(digit, 0.0, BASE - 1.0)
    step = HALF // DIGITS
    low = digit[:step]
    for at in range(step, HALF, step):
        low = low * BASE + digit[at : at + step]
    return high, (low - 128.0).astype(BF16)


def decoded(ref):
    near = ref[:HALF, :].astype(F32)
    low = ref[HALF:CODED, :].astype(F32) + 128.0
    digits = []
    for _ in range(DIGITS - 1):
        rest = jnp.floor(low * (1.0 / BASE))
        digits.append(low - rest * BASE)
        low = rest
    digit = jnp.concatenate([low] + digits[::-1], axis=0)
    return near + power(near) * ((digit + (0.5 - 0.5 * BASE)) * (1.0 / (128.0 * BASE)))


def store_coded(ref, a):
    high, low = coded(a)
    ref[:HALF, :] = high
    ref[HALF:CODED, :] = low


def kernel(
    latents, keys, values, out_grad, out_saved, log_norm,
    share, key_grad, value_grad,
    kb, vb, saved, norms, mine, pack, terms, parts, reduce_in, z_in, key_stage, value_stage, weights_held, score_held,
    local_sem, token_sem, token_send, token_recv, pack_send, pack_recv,
    back_send, back_recv, reduce_send, reduce_recv, z_send, z_recv,
):
    z = lax.axis_index("dp")
    seat = lax.axis_index("seq")
    core = seat % 2
    chip = seat // 2
    x, y = chip // SIDE, chip % SIDE
    parity = chip % 2
    other = (z, chip * 2 + (1 - core))

    def head_at(step, of_core):
        code = lax.shift_right_logical(jnp.int32(WORD), jnp.int32(step) * 4) % 8
        row = (y // 2 + code // SIDE) % 2
        return ((x + SIDE - code % SIDE) % SIDE) * SIDE + of_core + 2 * row

    def ahead(dx, dy):
        return ((x + dx) % SIDE) * SIDE + (y + dy) % SIDE

    def columns_of(head):
        return pl.ds(pl.multiple_of(head * DIM, DIM), DIM)

    def tokens_in(step):
        head = head_at(step, core)
        cut = columns_of(head)
        at = head // 2
        return (
            pltpu.make_async_copy(keys.at[:, cut], kb.at[0, at], token_sem.at[0, at]),
            pltpu.make_async_copy(values.at[:, cut], vb.at[0, at], token_sem.at[1, at]),
        )

    def tokens_over(step):
        head = head_at(step, 1 - core)
        cut = columns_of(head)
        at = head // 2
        return tuple(
            pltpu.make_async_remote_copy(
                src_ref=source.at[:, cut], dst_ref=target.at[1, at],
                send_sem=token_send.at[n, at], recv_sem=token_recv.at[n, at],
                device_id=other, device_id_type=MESH,
            )
            for n, (source, target) in enumerate(((keys, kb), (values, vb)))
        )

    small = [
        pltpu.make_async_copy(latents, mine.at[pl.ds(0, HALF)], local_sem.at[0]),
        pltpu.make_async_copy(out_grad, mine.at[pl.ds(HALF, HALF)], local_sem.at[1]),
        pltpu.make_async_copy(out_saved, saved, local_sem.at[2]),
        pltpu.make_async_copy(log_norm, norms, local_sem.at[3]),
    ]
    barrier = pltpu.get_barrier_semaphore()
    for dz in (4, 3, 5):
        pl.semaphore_signal(barrier, inc=1, device_id=((z + dz) % DEPTH, seat), device_id_type=MESH)
    for dx, dy in SENDS[::-1]:
        for flip in range(2):
            to = (z, ahead(dx, dy) * 2 + (core + flip) % 2)
            pl.semaphore_signal(barrier, inc=1, device_id=to, device_id_type=MESH)
    for dz in (2, 6, 1, 7):
        pl.semaphore_signal(barrier, inc=1, device_id=((z + dz) % DEPTH, seat), device_id_type=MESH)
    pl.semaphore_signal(barrier, inc=1, device_id=other, device_id_type=MESH)
    for copy in small:
        copy.start()

    for step in range(STEPS):
        for copy in tokens_in(step):
            copy.start()

    for copy in small:
        copy.wait()
    grads = mine[HALF : 2 * HALF, :].astype(F32)
    dots = jnp.sum(grads * saved[...].astype(F32), axis=0, keepdims=True)
    top = dots.astype(BF16).astype(F32)
    middle = (dots - top).astype(BF16).astype(F32)
    rest = dots - top - middle
    row = lax.broadcasted_iota(jnp.int32, (8, DIM), 0)
    rows = jnp.where(row == 0, top, jnp.where(row == 1, middle, jnp.where(row == 2, rest, 0.0)))
    mine[2 * HALF : ROWS, :] = rows.astype(BF16)

    pl.semaphore_wait(barrier, 2 * CHIPS - 1 + DEPTH - 1)

    def give(to):
        return pltpu.make_async_remote_copy(
            src_ref=mine, dst_ref=pack.at[chip // 2, core],
            send_sem=pack_send.at[to], recv_sem=pack_recv.at[chip // 2, core],
            device_id=(z, to * 2 + parity), device_id_type=MESH,
        )

    def given(at, half):
        return pltpu.make_async_remote_copy(
            src_ref=mine, dst_ref=pack.at[at, half],
            send_sem=pack_send.at[at], recv_sem=pack_recv.at[at, half],
            device_id=other, device_id_type=MESH,
        )

    @pl.when(parity != core)
    def _():
        give(chip).start()

    for dx, dy in SENDS:
        give(ahead(dx, dy)).start()
    for step in range(STEPS):
        for copy in tokens_over(step):
            copy.start()

    @pl.when(parity == core)
    def _():
        keep = pltpu.make_async_copy(mine, pack.at[chip // 2, core], local_sem.at[4])
        keep.start()
        keep.wait()

    def reduce(head, half):
        at = head // 2
        return pltpu.make_async_remote_copy(
            src_ref=parts.at[at, half], dst_ref=reduce_in.at[chip],
            send_sem=reduce_send.at[at, half], recv_sem=reduce_recv.at[chip],
            device_id=(z, head * 2 + half), device_id_type=MESH,
        )

    def reduced(sender):
        return pltpu.make_async_remote_copy(
            src_ref=parts.at[0, 0], dst_ref=reduce_in.at[sender],
            send_sem=reduce_send.at[0, 0], recv_sem=reduce_recv.at[sender],
            device_id=other, device_id_type=MESH,
        )

    def back(head):
        cut = columns_of(head)
        at = head // 2
        return tuple(
            pltpu.make_async_remote_copy(
                src_ref=source.at[at], dst_ref=target.at[:, cut],
                send_sem=back_send.at[n, at], recv_sem=back_recv.at[n, at],
                device_id=other, device_id_type=MESH,
            )
            for n, (source, target) in enumerate(
                ((key_stage, key_grad), (value_stage, value_grad))
            )
        )

    def both_halves(at):
        query = jnp.concatenate([pack[at, 0, :HALF, :], pack[at, 1, :HALF, :]], axis=0)
        grad = jnp.concatenate(
            [pack[at, 0, HALF : 2 * HALF, :], pack[at, 1, HALF : 2 * HALF, :]], axis=0
        )
        return query, grad

    def meet(step, carry):
        head = head_at(step, core)
        at = head // 2
        for half in range(2):
            @pl.when((head != chip) | (core != half))
            def _():
                given(at, half).wait_recv()

        query, grad = both_halves(at)
        dot_rows = pack[at, 0, 2 * HALF : ROWS, :].astype(F32)
        dot_rows += pack[at, 1, 2 * HALF : ROWS, :].astype(F32)
        row_dots = jnp.sum(dot_rows, axis=0, keepdims=True)
        norm = norms[pl.ds(head, 1), :] * LOG2E

        def scored(side):
            key = kb[side, at]
            scores = matmul(key, query, 1, 0)
            weight_grad = matmul(vb[side, at], grad, 1, 0)
            weights = jnp.exp2(scores * (SCALE * LOG2E) - norm)
            score_low = ((SCALE * weights) * (weight_grad - row_dots)).astype(BF16)
            return weights.astype(BF16), score_low, matmul(key, score_low, 0, 0)

        for copy in tokens_in(step):
            copy.wait()
        weights_low, score_low, term = scored(0)
        terms[...] = term
        weights_held[0, at] = weights_low
        score_held[0, at] = score_low

        for copy in tokens_over(step):
            copy.wait_recv()
        weights_low, score_low, term = scored(1)
        term += terms[...]
        store_coded(parts.at[at, 0], term[:HALF])
        store_coded(parts.at[at, 1], term[HALF:])
        for half in range(2):
            @pl.when((head != chip) | (core != half))
            def _():
                reduce(head, half).start()

        weights_held[1, at] = weights_low
        score_held[1, at] = score_low
        return carry

    def spread(step, carry):
        head = head_at(step, core)
        at = head // 2
        query, grad = both_halves(at)
        value_stage[at] = matmul(weights_held[1, at], grad, 1, 1).astype(BF16)
        key_stage[at] = matmul(score_held[1, at], query, 1, 1).astype(BF16)
        for copy in back(head):
            copy.start()
        cut = columns_of(head)
        value_grad[:, cut] = matmul(weights_held[0, at], grad, 1, 1).astype(BF16)
        key_grad[:, cut] = matmul(score_held[0, at], query, 1, 1).astype(BF16)
        return carry

    lax.fori_loop(0, STEPS, meet, 0)
    lax.fori_loop(0, EARLY, spread, 0)

    @pl.when(parity == core)
    def _():
        reduce_in[chip] = parts[chip // 2, core]

    @pl.when(parity != core)
    def _():
        reduced(chip).wait_recv()

    total = decoded(reduce_in.at[chip])
    for dx, dy in SENDS:
        sender = ahead(dx, dy)
        reduced(sender).wait_recv()
        total += decoded(reduce_in.at[sender])
    store_coded(z_in.at[z], total)

    def cross(to):
        return pltpu.make_async_remote_copy(
            src_ref=z_in.at[z], dst_ref=z_in.at[z],
            send_sem=z_send.at[to], recv_sem=z_recv.at[z],
            device_id=(to, seat), device_id_type=MESH,
        )

    def crossed(sender):
        return pltpu.make_async_remote_copy(
            src_ref=z_in.at[z], dst_ref=z_in.at[sender],
            send_sem=z_send.at[sender], recv_sem=z_recv.at[sender],
            device_id=(sender, seat), device_id_type=MESH,
        )

    for dz in (4, 3, 5, 2, 6, 1, 7):
        cross((z + dz) % DEPTH).start()
    lax.fori_loop(EARLY, STEPS, spread, 0)

    for step in range(STEPS):
        for copy in tokens_over(step):
            copy.wait_send()
        for copy in back(head_at(step, core)):
            copy.wait_send()
        for copy in back(head_at(step, 1 - core)):
            copy.wait_recv()
        head = head_at(step, core)
        for half in range(2):
            @pl.when((head != chip) | (core != half))
            def _():
                reduce(head, half).wait_send()
    for dx, dy in SENDS:
        give(ahead(dx, dy)).wait_send()

    @pl.when(parity != core)
    def _():
        give(chip).wait_send()

    for dz in (1, 7, 2, 6, 3, 5, 4):
        crossed((z + dz) % DEPTH).wait_recv()
    result = decoded(z_in.at[0])
    for at in range(1, DEPTH):
        result += decoded(z_in.at[at])
    share[...] = result
    for dz in range(1, DEPTH):
        cross((z + dz) % DEPTH).wait_send()


def finish(share, key_grad, value_grad, share_out, key_out, value_out, sem):
    copies = [pltpu.make_async_copy(share, share_out, sem.at[0])]
    width = key_grad.shape[1] // PIECES
    for n, (source, target) in enumerate(((key_grad, key_out), (value_grad, value_out))):
        for at in range(PIECES):
            cut = pl.ds(at * width, width)
            copies.append(
                pltpu.make_async_copy(source.at[:, cut], target.at[:, cut], sem.at[1 + n * PIECES + at])
            )
    for copy in copies:
        copy.start()
    for copy in copies:
        copy.wait()


def local(latents, saved_keys, saved_values, out_grad, out_saved, log_norm):
    tokens, width = saved_keys.shape[1:]
    dma = pltpu.SemaphoreType.DMA
    hbm = pl.BlockSpec(memory_space=pltpu.MemorySpace.HBM)
    vmem = pl.BlockSpec(memory_space=pltpu.MemorySpace.VMEM)
    held = [
        pltpu.with_memory_space_constraint(a, pltpu.MemorySpace.HBM)
        for a in (
            latents.T, saved_keys[0], saved_values[0], out_grad[0].T, out_saved[0].T, log_norm[0]
        )
    ]
    share, key_grad, value_grad = pl.pallas_call(
        kernel,
        name="resampler_backward",
        out_shape=(
            jax.ShapeDtypeStruct((HALF, LATENTS), F32),
            jax.ShapeDtypeStruct((tokens, width), BF16),
            jax.ShapeDtypeStruct((tokens, width), BF16),
        ),
        in_specs=[hbm] * 6,
        out_specs=(vmem, vmem, vmem),
        scratch_shapes=[
            pltpu.VMEM((2, STEPS, tokens, DIM), BF16),
            pltpu.VMEM((2, STEPS, tokens, DIM), BF16),
            pltpu.VMEM((HALF, LATENTS), BF16),
            pltpu.VMEM((HEADS, LATENTS), F32),
            pltpu.VMEM((ROWS, LATENTS), BF16),
            pltpu.VMEM((STEPS, 2, ROWS, LATENTS), BF16),
            pltpu.VMEM((DIM, LATENTS), F32),
            pltpu.VMEM((STEPS, 2, CODED, LATENTS), BF16),
            pltpu.VMEM((CHIPS, CODED, LATENTS), BF16),
            pltpu.VMEM((DEPTH, CODED, LATENTS), BF16),
            pltpu.VMEM((STEPS, tokens, DIM), BF16),
            pltpu.VMEM((STEPS, tokens, DIM), BF16),
            pltpu.VMEM((2, STEPS, tokens, DIM), BF16),
            pltpu.VMEM((2, STEPS, tokens, DIM), BF16),
            dma((5,)),
            dma((2, STEPS)), dma((2, STEPS)), dma((2, STEPS)),
            dma((CHIPS,)), dma((STEPS, 2)),
            dma((2, STEPS)), dma((2, STEPS)),
            dma((STEPS, 2)), dma((CHIPS,)),
            dma((DEPTH,)), dma((DEPTH,)),
        ],
        compiler_params=pltpu.CompilerParams(
            collective_id=0, has_side_effects=True, vmem_limit_bytes=40 << 20
        ),
    )(*held)
    share, key_grad, value_grad = pl.pallas_call(
        finish,
        name="results_out",
        out_shape=(
            jax.ShapeDtypeStruct((HALF, LATENTS), F32),
            jax.ShapeDtypeStruct((tokens, width), BF16),
            jax.ShapeDtypeStruct((tokens, width), BF16),
        ),
        in_specs=[vmem] * 3,
        out_specs=(hbm, hbm, hbm),
        scratch_shapes=[dma((1 + 2 * PIECES,))],
        compiler_params=pltpu.CompilerParams(vmem_limit_bytes=1 << 20),
    )(share, key_grad, value_grad)
    return share.T, key_grad[None], value_grad[None]


def solution(mesh):
    placed = (
        P(None, "seq"),
        P("dp", "seq", None),
        P("dp", "seq", None),
        P("dp", None, "seq"),
        P("dp", None, "seq"),
        P("dp", None, None),
    )
    return jax.shard_map(
        local,
        mesh=mesh,
        in_specs=placed,
        out_specs=(P(None, "seq"), P("dp", "seq", None), P("dp", "seq", None)),
        check_vma=False,
    )
```

```python
import jax
import jax.numpy as jnp
from jax import lax
from jax.experimental import pallas as pl
from jax.experimental.pallas import tpu as pltpu
from jax.sharding import PartitionSpec as P

HEADS = 16
DIM = 128
LATENTS = 128
HALF = DIM // 2
SCALE = DIM ** (-0.5)
LOG2E = 1.4426950408889634
SIDE = 4
CHIPS = SIDE * SIDE
DEPTH = 8
ROWS = 2 * HALF + 8
MESH = pl.DeviceIdType.MESH
BF16 = jnp.bfloat16
F32 = jnp.float32

SENDS = (
    (3, 0), (1, 0), (0, 3), (0, 1), (3, 1), (1, 3), (3, 3), (1, 1),
    (2, 0), (0, 2), (2, 3), (2, 1), (3, 2), (1, 2), (2, 2),
)
MEETS = ((0, 0), (0, 1), (1, 0), (1, 1), (3, 1), (2, 0), (2, 1), (3, 0))
WORD = sum((dx + SIDE * row) << (4 * at) for at, (dx, row) in enumerate(MEETS))
STEPS = len(MEETS)
PIECES = 16
EARLY = 6
BASE, DIGITS = 4, 4
CODED = HALF + HALF // DIGITS


def matmul(a, b, a_dim, b_dim):
    return lax.dot_general(
        a, b, (((a_dim,), (b_dim,)), ((), ())), preferred_element_type=F32
    )


def power(near):
    size = jnp.maximum(jnp.abs(near), 1e-30)
    return jnp.exp2(jnp.floor(jnp.log2(size) + 0.002))


def coded(a):
    high = a.astype(BF16)
    near = high.astype(F32)
    digit = jnp.floor((a - near) * ((128.0 * BASE) / power(near)) + 0.5 * BASE)
    digit = jnp.clip(digit, 0.0, BASE - 1.0)
    step = HALF // DIGITS
    low = digit[:step]
    for at in range(step, HALF, step):
        low = low * BASE + digit[at : at + step]
    return high, (low - 128.0).astype(BF16)


def decoded(ref):
    near = ref[:HALF, :].astype(F32)
    low = ref[HALF:CODED, :].astype(F32) + 128.0
    digits = []
    for _ in range(DIGITS - 1):
        rest = jnp.floor(low * (1.0 / BASE))
        digits.append(low - rest * BASE)
        low = rest
    digit = jnp.concatenate([low] + digits[::-1], axis=0)
    return near + power(near) * ((digit + (0.5 - 0.5 * BASE)) * (1.0 / (128.0 * BASE)))


def store_coded(ref, a):
    high, low = coded(a)
    ref[:HALF, :] = high
    ref[HALF:CODED, :] = low


def kernel(
    latents, keys, values, out_grad, out_saved, log_norm,
    share, key_grad, value_grad,
    kb, vb, saved, norms, mine, pack, terms, parts, reduce_in, z_in, z_full, key_stage, value_stage, weights_held, score_held,
    local_sem, token_sem, token_send, token_recv, pack_send, pack_recv,
    back_send, back_recv, reduce_send, reduce_recv, z_send, z_recv,
):
    z = lax.axis_index("dp")
    seat = lax.axis_index("seq")
    core = seat % 2
    chip = seat // 2
    x, y = chip // SIDE, chip % SIDE
    parity = chip % 2
    other = (z, chip * 2 + (1 - core))

    def head_at(step, of_core):
        code = lax.shift_right_logical(jnp.int32(WORD), jnp.int32(step) * 4) % 8
        row = (y // 2 + code // SIDE) % 2
        return ((x + SIDE - code % SIDE) % SIDE) * SIDE + of_core + 2 * row

    def ahead(dx, dy):
        return ((x + dx) % SIDE) * SIDE + (y + dy) % SIDE

    def columns_of(head):
        return pl.ds(pl.multiple_of(head * DIM, DIM), DIM)

    def tokens_in(step):
        head = head_at(step, core)
        cut = columns_of(head)
        at = head // 2
        return (
            pltpu.make_async_copy(keys.at[:, cut], kb.at[0, at], token_sem.at[0, at]),
            pltpu.make_async_copy(values.at[:, cut], vb.at[0, at], token_sem.at[1, at]),
        )

    def tokens_over(step):
        head = head_at(step, 1 - core)
        cut = columns_of(head)
        at = head // 2
        return tuple(
            pltpu.make_async_remote_copy(
                src_ref=source.at[:, cut], dst_ref=target.at[1, at],
                send_sem=token_send.at[n, at], recv_sem=token_recv.at[n, at],
                device_id=other, device_id_type=MESH,
            )
            for n, (source, target) in enumerate(((keys, kb), (values, vb)))
        )

    small = [
        pltpu.make_async_copy(latents, mine.at[pl.ds(0, HALF)], local_sem.at[0]),
        pltpu.make_async_copy(out_grad, mine.at[pl.ds(HALF, HALF)], local_sem.at[1]),
        pltpu.make_async_copy(out_saved, saved, local_sem.at[2]),
        pltpu.make_async_copy(log_norm, norms, local_sem.at[3]),
    ]
    barrier = pltpu.get_barrier_semaphore()
    for dz in (4, 3, 5):
        pl.semaphore_signal(barrier, inc=1, device_id=((z + dz) % DEPTH, seat), device_id_type=MESH)
    for dx, dy in SENDS[::-1]:
        for flip in range(2):
            to = (z, ahead(dx, dy) * 2 + (core + flip) % 2)
            pl.semaphore_signal(barrier, inc=1, device_id=to, device_id_type=MESH)
    for dz in (2, 6, 1, 7):
        pl.semaphore_signal(barrier, inc=1, device_id=((z + dz) % DEPTH, seat), device_id_type=MESH)
    pl.semaphore_signal(barrier, inc=1, device_id=other, device_id_type=MESH)
    for copy in small:
        copy.start()

    for step in range(STEPS):
        for copy in tokens_in(step):
            copy.start()

    for copy in small:
        copy.wait()
    grads = mine[HALF : 2 * HALF, :].astype(F32)
    dots = jnp.sum(grads * saved[...].astype(F32), axis=0, keepdims=True)
    top = dots.astype(BF16).astype(F32)
    middle = (dots - top).astype(BF16).astype(F32)
    rest = dots - top - middle
    row = lax.broadcasted_iota(jnp.int32, (8, DIM), 0)
    rows = jnp.where(row == 0, top, jnp.where(row == 1, middle, jnp.where(row == 2, rest, 0.0)))
    mine[2 * HALF : ROWS, :] = rows.astype(BF16)

    pl.semaphore_wait(barrier, 2 * CHIPS - 1 + DEPTH - 1)

    def give(to):
        return pltpu.make_async_remote_copy(
            src_ref=mine, dst_ref=pack.at[chip // 2, core],
            send_sem=pack_send.at[to], recv_sem=pack_recv.at[chip // 2, core],
            device_id=(z, to * 2 + parity), device_id_type=MESH,
        )

    def given(at, half):
        return pltpu.make_async_remote_copy(
            src_ref=mine, dst_ref=pack.at[at, half],
            send_sem=pack_send.at[at], recv_sem=pack_recv.at[at, half],
            device_id=other, device_id_type=MESH,
        )

    @pl.when(parity != core)
    def _():
        give(chip).start()

    for dx, dy in SENDS:
        give(ahead(dx, dy)).start()
    for step in range(STEPS):
        for copy in tokens_over(step):
            copy.start()

    @pl.when(parity == core)
    def _():
        keep = pltpu.make_async_copy(mine, pack.at[chip // 2, core], local_sem.at[4])
        keep.start()
        keep.wait()

    def reduce(head, half):
        at = head // 2
        return pltpu.make_async_remote_copy(
            src_ref=parts.at[at, half], dst_ref=reduce_in.at[chip],
            send_sem=reduce_send.at[at, half], recv_sem=reduce_recv.at[chip],
            device_id=(z, head * 2 + half), device_id_type=MESH,
        )

    def reduced(sender):
        return pltpu.make_async_remote_copy(
            src_ref=parts.at[0, 0], dst_ref=reduce_in.at[sender],
            send_sem=reduce_send.at[0, 0], recv_sem=reduce_recv.at[sender],
            device_id=other, device_id_type=MESH,
        )

    def back(head):
        cut = columns_of(head)
        at = head // 2
        return tuple(
            pltpu.make_async_remote_copy(
                src_ref=source.at[at], dst_ref=target.at[:, cut],
                send_sem=back_send.at[n, at], recv_sem=back_recv.at[n, at],
                device_id=other, device_id_type=MESH,
            )
            for n, (source, target) in enumerate(
                ((key_stage, key_grad), (value_stage, value_grad))
            )
        )

    def both_halves(at):
        query = jnp.concatenate([pack[at, 0, :HALF, :], pack[at, 1, :HALF, :]], axis=0)
        grad = jnp.concatenate(
            [pack[at, 0, HALF : 2 * HALF, :], pack[at, 1, HALF : 2 * HALF, :]], axis=0
        )
        return query, grad

    def meet(step, carry):
        head = head_at(step, core)
        at = head // 2
        for half in range(2):
            @pl.when((head != chip) | (core != half))
            def _():
                given(at, half).wait_recv()

        query, grad = both_halves(at)
        dot_rows = pack[at, 0, 2 * HALF : ROWS, :].astype(F32)
        dot_rows += pack[at, 1, 2 * HALF : ROWS, :].astype(F32)
        row_dots = jnp.sum(dot_rows, axis=0, keepdims=True)
        norm = norms[pl.ds(head, 1), :] * LOG2E

        def scored(side):
            key = kb[side, at]
            scores = matmul(key, query, 1, 0)
            weight_grad = matmul(vb[side, at], grad, 1, 0)
            weights = jnp.exp2(scores * (SCALE * LOG2E) - norm)
            score_low = ((SCALE * weights) * (weight_grad - row_dots)).astype(BF16)
            return weights.astype(BF16), score_low, matmul(key, score_low, 0, 0)

        for copy in tokens_in(step):
            copy.wait()
        weights_low, score_low, term = scored(0)
        terms[...] = term
        weights_held[0, at] = weights_low
        score_held[0, at] = score_low

        for copy in tokens_over(step):
            copy.wait_recv()
        weights_low, score_low, term = scored(1)
        term += terms[...]
        store_coded(parts.at[at, 0], term[:HALF])
        store_coded(parts.at[at, 1], term[HALF:])
        for half in range(2):
            @pl.when((head != chip) | (core != half))
            def _():
                reduce(head, half).start()

        weights_held[1, at] = weights_low
        score_held[1, at] = score_low
        return carry

    def spread(step, carry):
        head = head_at(step, core)
        at = head // 2
        query, grad = both_halves(at)
        value_stage[at] = matmul(weights_held[1, at], grad, 1, 1).astype(BF16)
        key_stage[at] = matmul(score_held[1, at], query, 1, 1).astype(BF16)
        for copy in back(head):
            copy.start()
        cut = columns_of(head)
        value_grad[:, cut] = matmul(weights_held[0, at], grad, 1, 1).astype(BF16)
        key_grad[:, cut] = matmul(score_held[0, at], query, 1, 1).astype(BF16)
        return carry

    lax.fori_loop(0, STEPS, meet, 0)
    lax.fori_loop(0, EARLY, spread, 0)

    @pl.when(parity == core)
    def _():
        reduce_in[chip] = parts[chip // 2, core]

    @pl.when(parity != core)
    def _():
        reduced(chip).wait_recv()

    total = decoded(reduce_in.at[chip])
    for dx, dy in SENDS:
        sender = ahead(dx, dy)
        reduced(sender).wait_recv()
        total += decoded(reduce_in.at[sender])
    store_coded(z_in.at[z], total)

    def cross(to):
        return pltpu.make_async_remote_copy(
            src_ref=z_in.at[z], dst_ref=z_in.at[z],
            send_sem=z_send.at[to], recv_sem=z_recv.at[z],
            device_id=(to, seat), device_id_type=MESH,
        )

    def crossed(sender):
        return pltpu.make_async_remote_copy(
            src_ref=z_in.at[z], dst_ref=z_in.at[sender],
            send_sem=z_send.at[sender], recv_sem=z_recv.at[sender],
            device_id=(sender, seat), device_id_type=MESH,
        )

    for dz in (4, 3, 5, 2, 6, 1, 7):
        cross((z + dz) % DEPTH).start()
    lax.fori_loop(EARLY, STEPS, spread, 0)

    for step in range(STEPS):
        for copy in tokens_over(step):
            copy.wait_send()
        for copy in back(head_at(step, core)):
            copy.wait_send()
        for copy in back(head_at(step, 1 - core)):
            copy.wait_recv()
        head = head_at(step, core)
        for half in range(2):
            @pl.when((head != chip) | (core != half))
            def _():
                reduce(head, half).wait_send()
    for dx, dy in SENDS:
        give(ahead(dx, dy)).wait_send()

    @pl.when(parity != core)
    def _():
        give(chip).wait_send()

    z_full[z] = decoded(z_in.at[z])
    for dz in (1, 7, 2, 6, 3, 5, 4):
        sender = (z + dz) % DEPTH
        crossed(sender).wait_recv()
        z_full[sender] = decoded(z_in.at[sender])
    result = z_full[0]
    for at in range(1, DEPTH):
        result += z_full[at]
    share[...] = result
    for dz in range(1, DEPTH):
        cross((z + dz) % DEPTH).wait_send()


def finish(share, key_grad, value_grad, share_out, key_out, value_out, sem):
    copies = [pltpu.make_async_copy(share, share_out, sem.at[0])]
    width = key_grad.shape[1] // PIECES
    for n, (source, target) in enumerate(((key_grad, key_out), (value_grad, value_out))):
        for at in range(PIECES):
            cut = pl.ds(at * width, width)
            copies.append(
                pltpu.make_async_copy(source.at[:, cut], target.at[:, cut], sem.at[1 + n * PIECES + at])
            )
    for copy in copies:
        copy.start()
    for copy in copies:
        copy.wait()


def local(latents, saved_keys, saved_values, out_grad, out_saved, log_norm):
    tokens, width = saved_keys.shape[1:]
    dma = pltpu.SemaphoreType.DMA
    hbm = pl.BlockSpec(memory_space=pltpu.MemorySpace.HBM)
    vmem = pl.BlockSpec(memory_space=pltpu.MemorySpace.VMEM)
    held = [
        pltpu.with_memory_space_constraint(a, pltpu.MemorySpace.HBM)
        for a in (
            latents.T, saved_keys[0], saved_values[0], out_grad[0].T, out_saved[0].T, log_norm[0]
        )
    ]
    share, key_grad, value_grad = pl.pallas_call(
        kernel,
        name="resampler_backward",
        out_shape=(
            jax.ShapeDtypeStruct((HALF, LATENTS), F32),
            jax.ShapeDtypeStruct((tokens, width), BF16),
            jax.ShapeDtypeStruct((tokens, width), BF16),
        ),
        in_specs=[hbm] * 6,
        out_specs=(vmem, vmem, vmem),
        scratch_shapes=[
            pltpu.VMEM((2, STEPS, tokens, DIM), BF16),
            pltpu.VMEM((2, STEPS, tokens, DIM), BF16),
            pltpu.VMEM((HALF, LATENTS), BF16),
            pltpu.VMEM((HEADS, LATENTS), F32),
            pltpu.VMEM((ROWS, LATENTS), BF16),
            pltpu.VMEM((STEPS, 2, ROWS, LATENTS), BF16),
            pltpu.VMEM((DIM, LATENTS), F32),
            pltpu.VMEM((STEPS, 2, CODED, LATENTS), BF16),
            pltpu.VMEM((CHIPS, CODED, LATENTS), BF16),
            pltpu.VMEM((DEPTH, CODED, LATENTS), BF16),
            pltpu.VMEM((DEPTH, HALF, LATENTS), F32),
            pltpu.VMEM((STEPS, tokens, DIM), BF16),
            pltpu.VMEM((STEPS, tokens, DIM), BF16),
            pltpu.VMEM((2, STEPS, tokens, DIM), BF16),
            pltpu.VMEM((2, STEPS, tokens, DIM), BF16),
            dma((5,)),
            dma((2, STEPS)), dma((2, STEPS)), dma((2, STEPS)),
            dma((CHIPS,)), dma((STEPS, 2)),
            dma((2, STEPS)), dma((2, STEPS)),
            dma((STEPS, 2)), dma((CHIPS,)),
            dma((DEPTH,)), dma((DEPTH,)),
        ],
        compiler_params=pltpu.CompilerParams(
            collective_id=0, has_side_effects=True, vmem_limit_bytes=40 << 20
        ),
    )(*held)
    share, key_grad, value_grad = pl.pallas_call(
        finish,
        name="results_out",
        out_shape=(
            jax.ShapeDtypeStruct((HALF, LATENTS), F32),
            jax.ShapeDtypeStruct((tokens, width), BF16),
            jax.ShapeDtypeStruct((tokens, width), BF16),
        ),
        in_specs=[vmem] * 3,
        out_specs=(hbm, hbm, hbm),
        scratch_shapes=[dma((1 + 2 * PIECES,))],
        compiler_params=pltpu.CompilerParams(vmem_limit_bytes=1 << 20),
    )(share, key_grad, value_grad)
    return share.T, key_grad[None], value_grad[None]


def solution(mesh):
    placed = (
        P(None, "seq"),
        P("dp", "seq", None),
        P("dp", "seq", None),
        P("dp", None, "seq"),
        P("dp", None, "seq"),
        P("dp", None, None),
    )
    return jax.shard_map(
        local,
        mesh=mesh,
        in_specs=placed,
        out_specs=(P(None, "seq"), P("dp", "seq", None), P("dp", "seq", None)),
        check_vma=False,
    )
```
